32 devices in a mesh: grp: 4 (over y, core), ctx: 8 (over z, x).
Axes of the slice: x: 2, y: 2, z: 4, core: 2. Of those that a mesh axis runs over, the one named last changes fastest.
Arguments:
- queries: bfloat16 [64, 8192], P('grp'), may hold values from -250 to 250
- resident_key_cache: bfloat16 [64, 1024, 512], P('grp', 'ctx'), may hold values from -6 to 6
- resident_value_cache: bfloat16 [64, 1024, 512], P('grp', 'ctx'), may hold values from -6 to 6
- res_len: int32 [64], P('grp'), may hold values from 2 to 1024, as said below
- visual_page_pool: bfloat16 [4096, 2, 8, 512], P(('grp', 'ctx')), may hold values from -6 to 6
- recall_holder: int32 [8, 64, 16], P('ctx', 'grp'), may hold values from 0 to 31, all different within a row; in each aligned block of 16 rows (0 to 15, 16 to 31, ..., all dimensions but the last counted through in order) at most 16 rows name the same one
- recall_slot: int32 [8, 64, 16], P('ctx', 'grp'), may hold values from 0 to 127
- o_weight: bfloat16 [8192, 4096], P('ctx'), may hold values from -3 to 3
- residual: bfloat16 [64, 4096], P('grp'), may hold values from -60 to 60
- norm_gain: float32 [4096], replicated, may hold values from 0.5 to 1.5
- expert_ids: int32 [64, 8], P('grp'), may hold values from 0 to 31, all different within a row; in each aligned block of 16 rows (0 to 15, 16 to 31, ...) at most 4 rows name the same one
- expert_weights: float32 [64, 8], P('grp'), may hold values from 1 to 4
- w_gate: bfloat16 [32, 768, 4096], P(('grp', 'ctx')), may hold values from -0.09375 to 0.09375
- w_up: bfloat16 [32, 768, 4096], P(('grp', 'ctx')), may hold values from -0.09375 to 0.09375
- w_down: bfloat16 [32, 768, 4096], P(('grp', 'ctx')), may hold values from -0.21875 to 0.21875
Outputs:
- mixed: bfloat16 [64, 4096], P('grp', 'ctx')
The draws below stay inside these ranges and needn't reach their ends.
Inputs may be any that keep to these rules, and one draw needn't show every extreme that they name: `res_len`: some request has length 1024 and some has length 2. `recall_holder`: the 16 holders of one request on one index of ctx differ; among the rows of one device (one index of ctx, the 16 requests of one group) no holder is named by more than 16 requests, and in some device's rows one holder by exactly 16. `expert_ids`: the 8 experts of a token differ; among the 16 tokens of one group no expert is named more than 4 times, and in some group one expert exactly 4 times.
All inputs are finite; a program needn't handle non-finite values.
Results may differ from the reference program's by a relative error of at most 0.025.
Values may be sent and summed in bfloat16 or wider, within the bound.
A program may use at most 128 MiB of HBM per device.

```python
import math
import jax
import jax.numpy as jnp
import numpy as np
from jax import lax

D = 4096
QUERY_HEADS = 64
KEY_VALUE_HEADS = 4
HEAD_WIDTH = 128
EFF = 768
TOPK = 8
CAPE = 4
PAGE_TOKENS = 8
PG_DEV = 16
REQ = 16
EXPERTS = 32
PARTS_SIZE = 1
EPART = 768
REQUEST_COUNT = 64
CONTEXT_LENGTH = 1024
CAP = 16
PAGES_PER_UNIT = 128
N_CTX = 8
DEVICES = 32


def draw_queries(key, part):
    start_offset = jax.random.truncated_normal(jax.random.fold_in(key, 6), -6.0, 6.0, (REQUEST_COUNT, KEY_VALUE_HEADS, QUERY_HEADS // KEY_VALUE_HEADS, HEAD_WIDTH), jnp.float32)
    return start_offset.reshape(REQUEST_COUNT, QUERY_HEADS * HEAD_WIDTH).astype(jnp.bfloat16)


def draw_resident_key_cache(key, part):
    random_noise = jax.random.truncated_normal(jax.random.fold_in(key, 5), -6.0, 6.0, (REQUEST_COUNT, CONTEXT_LENGTH, KEY_VALUE_HEADS * HEAD_WIDTH), jnp.float32)
    return random_noise.astype(jnp.bfloat16)


def draw_residual(key, part):
    start_offset = jax.random.truncated_normal(jax.random.fold_in(key, 31), -4.0, 4.0, (REQUEST_COUNT, D), jnp.float32)
    return start_offset.astype(jnp.bfloat16)


def draw_res_len(key, part):
    lengths = jax.random.randint(jax.random.fold_in(key, 21), (REQUEST_COUNT,), 2, CONTEXT_LENGTH + 1)
    chosen = jax.random.randint(jax.random.fold_in(key, 22), (), 0, REQUEST_COUNT)
    lengths = lengths.at[chosen].set(CONTEXT_LENGTH)
    lengths = lengths.at[(chosen + REQUEST_COUNT // 2) % REQUEST_COUNT].set(2)
    return lengths.astype(jnp.int32)


def set_ends(array, key, smallest, high):
    longest = array.shape.index(max(array.shape))
    spots = []
    for shift in (0, 1):
        where = [jax.random.randint(jax.random.fold_in(key, axis), (), 0, length) for axis, length in enumerate(array.shape)]
        where[longest] = (where[longest] + shift) % array.shape[longest]
        spots.append(tuple(where))
    return array.at[spots[0]].set(smallest).at[spots[1]].set(high)


def shard_levels(rng, shape, pieces, smallest, largest):
    def one(dim, shards_of):
        steps = jax.random.uniform(jax.random.fold_in(jax.random.fold_in(rng, 6), dim), (shards_of,), jnp.float32, smallest / len(pieces), largest / len(pieces))
        return jnp.repeat(jnp.exp(steps), shape[dim] // shards_of).reshape((-1,) + (1,) * (len(shape) - dim - 1))

    level = one(*pieces[0])
    for cut in pieces[1:]:
        level = level * one(*cut)
    return level


def assign_block(own_key, own, number, rows, count, top, reach, slope):
    ranking = jax.random.permutation(own_key, count)
    heavy_load, common = load_shares(count, rows * top, reach, slope, True), load_shares(count, rows * top, reach, slope, False)
    places = jnp.arange(count)

    def named(sizes, rotation):
        used = int((sizes > 0).sum())
        fixed = max(1, used // 4)
        shifted = fixed + (places - fixed + rotation * (used - fixed)) % max(1, count - fixed)
        return jnp.zeros((count,), jnp.int32).at[ranking[jnp.where(places < fixed, places, shifted)]].set(jnp.asarray(sizes, jnp.int32))

    sizes = jnp.where(number % 4 == 0, named(heavy_load, number // 4), named(common, number - number // 4 - 1))
    mixed = jax.random.permutation(jax.random.fold_in(own, 3), count)
    donor, taker = mixed[0:count // 2 * 2:2], mixed[1:count // 2 * 2:2]
    margin = jnp.minimum(sizes[donor] - 1, reach - sizes[taker]) // 2
    margin = jnp.where((donor == ranking[0]) | (taker == ranking[0]) | (sizes[taker] == 0), 0, jnp.maximum(margin, 0))
    shifted = jax.random.randint(jax.random.fold_in(own, 4), (count // 2,), 0, 1 << 20) % (margin + 1)
    sizes = sizes.at[donor].add(-shifted).at[taker].add(shifted)
    labels = jnp.searchsorted(jnp.cumsum(sizes), jnp.arange(rows * top), side="right").astype(jnp.int32)
    table = labels.reshape(top, rows).T
    table = table[jax.random.permutation(jax.random.fold_in(own, 1), rows)]
    rotation = jax.random.randint(jax.random.fold_in(own, 2), (rows, 1), 0, top)
    return jnp.take_along_axis(table, (jnp.arange(top)[None, :] + rotation) % top, axis=1)


def load_shares(count, total, reach, lean, full):
    portions = [(1 << 20) // math.isqrt(grade ** lean) + 1 for grade in range(1, count + 1)]
    largest = reach if full else min(reach, max(-(-total // count), total * portions[0] // sum(portions)))
    least = 1 if total - largest >= count - 1 else 0
    counts, surplus = [largest] + [least] * (count - 1), total - largest - least * (count - 1)
    while surplus > 0:
        movable = [i for i in range(1, count) if counts[i] < largest] or [i for i in range(1, count) if counts[i] < reach]
        mass, left = sum([portions[i] for i in movable]), surplus
        for i in movable:
            more = min(reach - counts[i], max(1, left * portions[i] // mass), surplus)
            counts[i] = counts[i] + more
            surplus = surplus - more
    return np.array(counts)


def centred(key, extent, deviation, limit, cuts=(), kind=jnp.bfloat16):
    entries = jax.random.normal(key, extent, jnp.float32) * deviation
    if len(cuts) > 0:
        entries = shard_levels(key, extent, cuts, -0.22, 0.18) * entries
    return jnp.clip(entries, min=-limit, max=limit).astype(kind)


def setup_inputs(seed: int = 0) -> dict:
    splits = jax.random.split(jax.random.key(seed), 16)
    queries = draw_queries(jax.random.fold_in(splits[15], 71), 0)
    resident_key_cache = draw_resident_key_cache(jax.random.fold_in(splits[15], 71), 0)
    resident_value_cache = centred(splits[2], (REQUEST_COUNT, CONTEXT_LENGTH, KEY_VALUE_HEADS * HEAD_WIDTH), 1.0, 6.0, ((0, 4), (1, 8)))
    res_len = draw_res_len(jax.random.fold_in(splits[15], 71), 0)
    visual_page_pool = centred(splits[4], (DEVICES * PAGES_PER_UNIT, 2, PAGE_TOKENS, KEY_VALUE_HEADS * HEAD_WIDTH), 1.0, 6.0, ((0, 32),))
    recall_holder_keys = jax.random.split(jax.random.fold_in(splits[5], 1), N_CTX * REQUEST_COUNT // REQ)
    recall_holder_turns = jax.random.permutation(jax.random.fold_in(splits[5], 3), N_CTX * REQUEST_COUNT // REQ)
    recall_holder = jax.vmap(lambda own, number: assign_block(jax.random.fold_in(splits[5], 2), own, number, REQ, DEVICES, PG_DEV, CAP, 2))(recall_holder_keys, recall_holder_turns).reshape((N_CTX, REQUEST_COUNT, PG_DEV))
    recall_slot = set_ends(jax.random.randint(splits[6], (N_CTX, REQUEST_COUNT, PG_DEV), 0, PAGES_PER_UNIT), jax.random.fold_in(splits[6], 1), 0, PAGES_PER_UNIT - 1).astype(jnp.int32)
    o_weight = centred(splits[7], (QUERY_HEADS * HEAD_WIDTH, D), 0.5, 3.0, ((0, 8),))
    residual = draw_residual(jax.random.fold_in(splits[15], 71), 0)
    norm_gain = jnp.clip(jax.random.uniform(splits[9], (D,), jnp.float32, 0.5, 1.5), 0.5, 1.5)
    expert_ids_keys = jax.random.split(jax.random.fold_in(splits[10], 1), REQUEST_COUNT // REQ)
    expert_ids_turns = jax.random.permutation(jax.random.fold_in(splits[10], 3), REQUEST_COUNT // REQ)
    expert_ids = jax.vmap(lambda own, number: assign_block(jax.random.fold_in(splits[10], 2), own, number, REQ, EXPERTS, TOPK, CAPE, 1))(expert_ids_keys, expert_ids_turns).reshape((REQUEST_COUNT, TOPK))
    expert_weights = jnp.clip(jnp.exp(math.log(4.0) - 1.3862944 * jax.random.uniform(splits[11], (REQUEST_COUNT, TOPK), jnp.float32) ** shard_levels(splits[11], (REQUEST_COUNT, TOPK), ((0, 4),), -0.2, 0.2)), 1.0, 4.0)
    w_gate = centred(splits[12], (EXPERTS * PARTS_SIZE, EPART, D), D ** -0.5, 0.09375, ((0, 32),))
    w_up = centred(splits[13], (EXPERTS * PARTS_SIZE, EPART, D), D ** -0.5, 0.09375, ((0, 32),))
    w_down = centred(splits[14], (EXPERTS * PARTS_SIZE, EPART, D), EFF ** -0.5, 0.21875, ((0, 32),))
    return dict(queries=queries, resident_key_cache=resident_key_cache, resident_value_cache=resident_value_cache, res_len=res_len, visual_page_pool=visual_page_pool, recall_holder=recall_holder, recall_slot=recall_slot, o_weight=o_weight, residual=residual, norm_gain=norm_gain, expert_ids=expert_ids, expert_weights=expert_weights, w_gate=w_gate, w_up=w_up, w_down=w_down)


VERY_NEGATIVE = -1e+30

def reference(queries, resident_key_cache, resident_value_cache, res_len, visual_page_pool, recall_holder, recall_slot, o_weight, residual, norm_gain, expert_ids, expert_weights, w_gate, w_up, w_down):
    head_groups = QUERY_HEADS // KEY_VALUE_HEADS
    score_scale = HEAD_WIDTH ** (-0.5)
    positions = jnp.arange(CONTEXT_LENGTH, dtype=jnp.int32)
    recall_count = N_CTX * PG_DEV * PAGE_TOKENS

    def attend(token_position):
        query_matrix = queries[token_position].reshape(KEY_VALUE_HEADS, head_groups, HEAD_WIDTH).astype(jnp.float32)
        page_ids = (recall_holder[:, token_position, :] * PAGES_PER_UNIT + recall_slot[:, token_position, :]).reshape(-1).astype(jnp.int32)
        page_row_list = jnp.take(visual_page_pool, page_ids, axis=0)
        joined_keys = jnp.concatenate([resident_key_cache[token_position], page_row_list[:, 0].reshape(recall_count, KEY_VALUE_HEADS * HEAD_WIDTH)], axis=0)
        joined_values = jnp.concatenate([resident_value_cache[token_position], page_row_list[:, 1].reshape(recall_count, KEY_VALUE_HEADS * HEAD_WIDTH)], axis=0)
        is_valid = jnp.concatenate([positions < res_len[token_position], jnp.ones((recall_count,), dtype=bool)])
        expanded_keys = joined_keys.reshape(-1, KEY_VALUE_HEADS, HEAD_WIDTH).astype(jnp.float32)
        expanded_values = joined_values.reshape(-1, KEY_VALUE_HEADS, HEAD_WIDTH).astype(jnp.float32)
        scores = jnp.einsum('kgd,nkd->kgn', query_matrix, expanded_keys) * score_scale
        scores = jnp.where(is_valid[None, None, :], scores, VERY_NEGATIVE)
        weights = jnp.exp(scores - lax.optimization_barrier(jnp.max(scores, axis=-1, keepdims=True)))
        weights = jnp.where(is_valid[None, None, :], weights, 0.0)
        row_total = lax.optimization_barrier(jnp.sum(weights, axis=-1))
        rounded = lax.optimization_barrier(weights.astype(jnp.bfloat16)).astype(jnp.float32)
        weighted_sum = jnp.einsum('kgn,nkd->kgd', rounded, expanded_values)
        return (weighted_sum / row_total[..., None]).astype(jnp.bfloat16).reshape(QUERY_HEADS * HEAD_WIDTH)
    attention = lax.map(attend, jnp.arange(REQUEST_COUNT, dtype=jnp.int32))
    projected = jnp.dot(attention, o_weight, preferred_element_type=jnp.float32)
    hidden = residual.astype(jnp.float32) + projected
    normed = (hidden * lax.rsqrt(lax.optimization_barrier(jnp.mean(hidden * hidden, axis=-1, keepdims=True)) + 1e-06) * norm_gain).astype(jnp.bfloat16)
    pair_token = jnp.arange(REQUEST_COUNT * TOPK, dtype=jnp.int32) // TOPK
    pair_expert = expert_ids.reshape(-1).astype(jnp.int32)
    part_rows = PARTS_SIZE * EPART

    def run_pair(pair_items):
        token_position, expert = pair_items
        first_row = (expert * PARTS_SIZE).astype(jnp.int32)
        gate_rows = lax.dynamic_slice_in_dim(w_gate, first_row, PARTS_SIZE, 0).reshape(part_rows, D)
        up_rows = lax.dynamic_slice_in_dim(w_up, first_row, PARTS_SIZE, 0).reshape(part_rows, D)
        down_rows = lax.dynamic_slice_in_dim(w_down, first_row, PARTS_SIZE, 0).reshape(part_rows, D)
        vector = normed[token_position]
        gate_value = jnp.dot(gate_rows, vector, preferred_element_type=jnp.float32)
        upward = jnp.dot(up_rows, vector, preferred_element_type=jnp.float32)
        activation = (jax.nn.silu(gate_value) * upward).astype(jnp.bfloat16)
        return jnp.dot(activation, down_rows, preferred_element_type=jnp.float32)
    outputs = lax.map(run_pair, (pair_token, pair_expert))
    mixture = lax.optimization_barrier(jnp.sum(outputs.reshape(REQUEST_COUNT, TOPK, D) * expert_weights[..., None], axis=1))
    return (hidden + mixture).astype(jnp.bfloat16)
```

```python
import functools

import jax
import jax.numpy as jnp
from jax import lax
from jax.experimental import pallas as pl
from jax.experimental.pallas import tpu as pltpu
from jax.sharding import PartitionSpec as P

KEY_VALUE_HEADS = 4
HEAD_WIDTH = 128
EXP_GRP = 8
LANES = 128
CAPE = 4
PARTS_APART = 32
EARLY = 4

VERY_NEGATIVE = -1e30
NORM_EPSILON = 1e-06
LOG2E = 1.4426950408889634
SCALE = HEAD_WIDTH ** (-0.5)

NT = (((1,), (1,)), ((), ()))
F32 = jnp.float32
BF16 = jnp.bfloat16


def wait_bytes(ref, sem):
    pltpu.make_async_copy(ref, ref, sem).wait()


def kernel(
    grp_count,
    ctx_count,
    page_tokens,
    q_hbm,
    kc_hbm,
    vc_hbm,
    rl_ref,
    pool_hbm,
    holder_ref,
    slot_ref,
    ow_hbm,
    res_ref,
    gain_ref,
    ids_ref,
    ew_ref,
    wg_hbm,
    wu_hbm,
    wd_hbm,
    out_ref,
    q_all,
    qt,
    kc,
    vc,
    pk,
    pv,
    ow,
    wg,
    wu,
    wd,
    turn,
    named,
    msg_ref,
    idx_recv,
    bias,
    o_res,
    l_res,
    yo_send,
    yo_recv,
    o_send,
    o_recv,
    mix_w,
    p_send,
    p_recv,
    x_send,
    x_recv,
    xs,
    y_send,
    y_recv,
    ys,
    local_sem,
    q_send_sem,
    q_recv_sem,
    pool_send_sem,
    pool_recv_sem,
    yo_send_sem,
    yo_recv_sem,
    send_sem,
    recv_sem,
):
    n = grp_count * ctx_count
    my_g = lax.axis_index("grp")
    my_c = lax.axis_index("ctx")
    me = my_g * ctx_count + my_c
    y_count = grp_count // 2
    my_y = my_g // 2
    my_core = lax.rem(my_g, 2)
    pair = (my_g + 1 - 2 * my_core, my_c)
    req = q_all.shape[1]
    heads = qt.shape[1]
    per_kv = heads // KEY_VALUE_HEADS
    own_width = o_send.shape[2] - LANES
    heads_each = own_width // HEAD_WIDTH
    c_per_kv = per_kv // heads_each
    page_count = pk.shape[1]
    tokens = page_count * page_tokens
    columns = p_send.shape[2]
    same_core = y_count * ctx_count
    mine = my_y * ctx_count + my_c

    def dev(d):
        return (d // ctx_count, lax.rem(d, ctx_count))

    def far_first(k, count, at):
        above, below = count - 1 - at, at
        most, least = jnp.maximum(above, below), jnp.minimum(above, below)
        lead = most - least
        j = jnp.maximum(k - lead, 0)
        side = jnp.where(above >= below, 1, -1) * (1 - 2 * lax.rem(j, 2))
        return at + side * jnp.where(k < lead, most - k, least - j // 2)

    loads = [
        (kc_hbm, kc),
        (vc_hbm, vc),
        (q_hbm, q_all.at[my_y]),
        (pool_hbm.at[:, 0], pk.at[my_core]),
        (pool_hbm.at[:, 1], pv.at[my_core]),
        (ow_hbm, ow),
        (wg_hbm.at[0], wg),
        (wu_hbm.at[0], wu),
        (wd_hbm.at[0], wd),
    ]
    copies = [pltpu.make_async_copy(s, d, local_sem.at[i]) for i, (s, d) in enumerate(loads)]
    for copy in copies[:5]:
        copy.start()

    barrier = pltpu.get_barrier_semaphore()

    @pl.loop(1, n)
    def _(k):
        pl.semaphore_signal(
            barrier, inc=1, device_id=dev(lax.rem(me + k, n)), device_id_type=pl.DeviceIdType.MESH
        )

    lists = holder_ref.shape[1]
    for i, ref in enumerate((holder_ref, slot_ref)):
        turn[i] = jnp.zeros((LANES, LANES), F32)
        for r in range(3):
            turn[i, r * req : (r + 1) * req, 0:lists] = ref[...].astype(F32)
    holder_t = turn[0].T
    slot_t = turn[1].T
    holder_id = lax.broadcasted_iota(jnp.int32, (n, LANES), 0).astype(F32)
    table = jnp.zeros((n, LANES), F32)
    for j in range(lists):
        table = table + jnp.where(
            holder_t[j : j + 1, :] == holder_id, slot_t[j : j + 1, :] + 1.0, 0.0
        )
    named[...] = table

    @pl.loop(0, same_core)
    def _(i):
        first = (i // ctx_count) * 2 * ctx_count + lax.rem(i, ctx_count)
        msg_ref[i, 0:1, :] = named[pl.ds(first, 1), :]
        msg_ref[i, 1:2, :] = named[pl.ds(first + ctx_count, 1), :]

    rows_here = kc.shape[1]

    def resident(t, carry):
        pos = my_c * rows_here + lax.broadcasted_iota(jnp.int32, (heads, rows_here), 1)
        ok = pos < rl_ref[t]
        s = jnp.concatenate(
            [
                lax.dot_general(
                    qt[t, k * per_kv : (k + 1) * per_kv, :].astype(BF16),
                    kc[t, :, k * HEAD_WIDTH : (k + 1) * HEAD_WIDTH],
                    NT,
                    preferred_element_type=F32,
                )
                for k in range(KEY_VALUE_HEADS)
            ],
            axis=0,
        )
        s = jnp.where(ok, s, VERY_NEGATIVE)
        m = jnp.max(s, axis=1, keepdims=True)
        p = jnp.exp2((s - m) * (SCALE * LOG2E))
        p = jnp.where(ok, p, 0.0)
        total = jnp.maximum(jnp.sum(p, axis=1, keepdims=True), 1e-30)
        pb = p.astype(BF16)
        o = jnp.concatenate(
            [
                jnp.dot(
                    pb[k * per_kv : (k + 1) * per_kv, :],
                    vc[t, :, k * HEAD_WIDTH : (k + 1) * HEAD_WIDTH],
                    preferred_element_type=F32,
                )
                for k in range(KEY_VALUE_HEADS)
            ],
            axis=0,
        )
        o_res[t] = o / total
        lse = m * (SCALE * LOG2E) + jnp.log(total) * LOG2E
        l_res[t] = jnp.broadcast_to(lse, (heads, LANES))
        return carry

    copies[0].wait()
    copies[1].wait()
    copies[2].wait()
    for h in range(heads):
        qt[:, h, :] = q_all[my_y, :, h * HEAD_WIDTH : (h + 1) * HEAD_WIDTH].astype(F32)
    lax.fori_loop(0, EARLY, resident, 0, unroll=4)

    pl.semaphore_wait(barrier, n - 1)

    def send(src, dst, s_sem, r_sem, target):
        pltpu.make_async_remote_copy(
            src_ref=src,
            dst_ref=dst,
            send_sem=s_sem,
            recv_sem=r_sem,
            device_id=target,
            device_id_type=pl.DeviceIdType.MESH,
        ).start()

    for i in range(2):
        send(
            pool_hbm.at[:, i],
            (pk, pv)[i].at[my_core],
            pool_send_sem.at[i],
            pool_recv_sem.at[i],
            pair,
        )

    @pl.loop(1, same_core)
    def _(k):
        i = lax.rem(mine + k, same_core)
        send(
            msg_ref.at[i],
            idx_recv.at[mine],
            send_sem.at[0],
            recv_sem.at[0],
            ((i // ctx_count) * 2 + my_core, lax.rem(i, ctx_count)),
        )

    for k in range(1, y_count):
        y = lax.rem(my_y + k, y_count)
        send(q_hbm, q_all.at[my_y], q_send_sem, q_recv_sem.at[my_y], (y * 2 + my_core, my_c))

    for copy in copies[5:]:
        copy.start()

    idx_recv[mine] = msg_ref[mine]
    lax.fori_loop(EARLY, req, resident, 0, unroll=4)

    wait_bytes(idx_recv.at[pl.ds(0, same_core - 1)], recv_sem.at[0])
    lane = lax.broadcasted_iota(jnp.int32, (page_count, LANES), 1)
    page_id = (lax.broadcasted_iota(jnp.int32, (page_count, LANES), 0) + 1).astype(F32)
    spread = (
        lax.broadcasted_iota(jnp.int32, (tokens, page_count), 0) // page_tokens
        == lax.broadcasted_iota(jnp.int32, (tokens, page_count), 1)
    ).astype(F32).astype(BF16)

    @pl.loop(0, y_count)
    def _(y):
        for core in range(2):
            def add(c, count):
                row = idx_recv[y * ctx_count + c, core : core + 1, :]
                return count + (jnp.broadcast_to(row, page_id.shape) == page_id).astype(F32)

            count = lax.fori_loop(0, ctx_count, add, jnp.zeros((page_count, LANES), F32), unroll=8)
            level = jnp.where(
                count > 0.0, jnp.log(jnp.maximum(count, 1.0)) * (1.0 / SCALE), VERY_NEGATIVE
            )
            hi = level.astype(BF16).astype(F32)
            rest = jnp.where(count > 0.0, level - hi, 0.0)
            mid = rest.astype(BF16).astype(F32)
            low = rest - mid
            part = jnp.where(lane < req, hi, jnp.where(lane < 2 * req, mid, low))
            part = jnp.where(lane < 3 * req, part, 0.0).astype(BF16)
            bias[y, core * tokens : (core + 1) * tokens, :] = jnp.dot(
                spread, part, preferred_element_type=F32
            ).astype(BF16)

    copies[3].wait()
    copies[4].wait()
    wait_bytes(pk.at[0], pool_recv_sem.at[0])
    wait_bytes(pv.at[0], pool_recv_sem.at[1])
    rows = per_kv * req
    row_t = lax.rem(lax.broadcasted_iota(jnp.int32, (rows, LANES), 0), req)
    row_lane = lax.broadcasted_iota(jnp.int32, (rows, LANES), 1)
    chooser = (
        ((lax.rem(row_lane, req) == row_t) & (row_lane < 3 * req)).astype(F32).astype(BF16)
    )
    st_lane = lax.broadcasted_iota(jnp.int32, (req, LANES), 1)

    def encode(stat):
        hi = stat.astype(BF16).astype(F32)
        rest = stat - hi
        mid = rest.astype(BF16).astype(F32)
        low = rest - mid
        return (hi + pltpu.roll(mid, PARTS_APART, 1) + pltpu.roll(low, 2 * PARTS_APART, 1)).astype(BF16)

    def decode(block):
        x = block.astype(F32)
        return (
            x + pltpu.roll(x, LANES - PARTS_APART, 1) + pltpu.roll(x, LANES - 2 * PARTS_APART, 1)
        )

    def pool_part(y, kv):
        qk = jnp.concatenate(
            [
                q_all[
                    y,
                    :,
                    pl.ds(pl.multiple_of((kv * per_kv + h) * HEAD_WIDTH, HEAD_WIDTH), HEAD_WIDTH),
                ]
                for h in range(per_kv)
            ],
            axis=0,
        )
        kv_cols = pl.ds(pl.multiple_of(kv * HEAD_WIDTH, HEAD_WIDTH), HEAD_WIDTH)
        qa = jnp.concatenate([qk, chooser], axis=1)
        ka = jnp.concatenate(
            [pk[:, :, :, kv_cols].reshape(2 * tokens, HEAD_WIDTH), bias[y]], axis=1
        )
        s = lax.dot_general(qa, ka, NT, preferred_element_type=F32)
        m = jnp.max(s, axis=1, keepdims=True)
        p = jnp.exp2((s - m) * (SCALE * LOG2E)).astype(BF16)
        va = jnp.concatenate(
            [
                pv[:, :, :, kv_cols].reshape(2 * tokens, HEAD_WIDTH),
                jnp.ones((2 * tokens, LANES), BF16),
            ],
            axis=1,
        )
        o = jnp.dot(p, va, preferred_element_type=F32)
        top = jnp.broadcast_to(m * (SCALE * LOG2E), (rows, LANES))
        return o[:, :HEAD_WIDTH], o[:, HEAD_WIDTH:], top

    def of_head(x, h):
        return x[h * req : (h + 1) * req, :]

    @pl.loop(1, y_count)
    def _(k):
        y = lax.rem(my_y + k, y_count)
        wait_bytes(q_all.at[y], q_recv_sem.at[y])
        for kv in range(KEY_VALUE_HEADS):
            o, total, top = pool_part(y, kv)
            o = o / total
            lse = top + jnp.log(total) * LOG2E
            stat = jnp.zeros((req, LANES), F32)
            for h in range(per_kv):
                yo_send[kv, y, :, h * HEAD_WIDTH : (h + 1) * HEAD_WIDTH] = of_head(o, h).astype(BF16)
                stat = jnp.where(st_lane == h, of_head(lse, h), stat)
            yo_send[kv, y, :, per_kv * HEAD_WIDTH :] = encode(stat)
            send(
                yo_send.at[kv, y],
                yo_recv.at[kv, my_y],
                yo_send_sem.at[kv],
                yo_recv_sem.at[kv],
                (y * 2 + my_core, my_c),
            )

    my_kv = my_c // c_per_kv
    for i in range(KEY_VALUE_HEADS):
        kv = far_first(i, KEY_VALUE_HEADS, my_kv)
        o, total, top = pool_part(my_y, kv)
        wait_bytes(yo_recv.at[kv, pl.ds(0, y_count - 1)], yo_recv_sem.at[kv])
        others = []
        for k in range(1, y_count):
            y = lax.rem(my_y + k, y_count)
            others.append((y, decode(yo_recv[kv, y, :, per_kv * HEAD_WIDTH :])))
        for b in range(c_per_kv):
            c = kv * c_per_kv + b
            stat = jnp.zeros((req, LANES), F32)
            for j in range(heads_each):
                h = b * heads_each + j
                terms = [
                    (of_head(top, h), of_head(total, h), of_head(o, h)),
                    (l_res[:, kv * per_kv + h, :], None, o_res[:, kv * per_kv + h, :]),
                ]
                for y, l_y in others:
                    o_y = yo_recv[kv, y, :, h * HEAD_WIDTH : (h + 1) * HEAD_WIDTH].astype(F32)
                    terms.append((jnp.broadcast_to(l_y[:, h : h + 1], (req, LANES)), None, o_y))
                best = functools.reduce(jnp.maximum, [t[0] for t in terms])
                weights = [jnp.exp2(t[0] - best) for t in terms]
                mass = sum(w if t[1] is None else w * t[1] for w, t in zip(weights, terms))
                o_h = sum(w * t[2] for w, t in zip(weights, terms)) / mass
                l_h = best + jnp.log(mass) * LOG2E
                o_send[c, :, j * HEAD_WIDTH : (j + 1) * HEAD_WIDTH] = o_h.astype(BF16)
                stat = jnp.where(st_lane == j, l_h, stat)
            o_send[c, :, own_width:] = encode(stat)
        last = i == KEY_VALUE_HEADS - 1
        for b in range(1 if last else 0, c_per_kv):
            c = kv * c_per_kv + (lax.rem(my_c + b, c_per_kv) if last else b)
            send(o_send.at[c], o_recv.at[my_c], send_sem.at[1], recv_sem.at[1], (my_g, c))

    o_recv[my_c] = o_send[my_c]
    wait_bytes(o_recv.at[pl.ds(0, ctx_count - 1)], recv_sem.at[1])

    def highest(i, top):
        level = decode(o_recv[i, :, own_width:])
        mix_w[i] = level
        return jnp.maximum(top, level)

    top = lax.fori_loop(0, ctx_count, highest, jnp.full((req, LANES), -3e38, F32), unroll=8)

    def weigh(i, total):
        w = jnp.exp2(mix_w[i] - top)
        mix_w[i] = w
        return total + w

    total = lax.fori_loop(0, ctx_count, weigh, jnp.zeros((req, LANES), F32), unroll=8)
    inverse = 1.0 / total

    def join(i, acc):
        w = mix_w[i] * inverse
        return tuple(
            acc[j]
            + w[:, j : j + 1] * o_recv[i, :, j * HEAD_WIDTH : (j + 1) * HEAD_WIDTH].astype(F32)
            for j in range(heads_each)
        )

    acc = lax.fori_loop(
        0,
        ctx_count,
        join,
        tuple(jnp.zeros((req, HEAD_WIDTH), F32) for _ in range(heads_each)),
        unroll=8,
    )
    attn = jnp.concatenate([a.astype(BF16) for a in acc], axis=1)

    copies[5].wait()

    def project(c):
        cols = pl.ds(pl.multiple_of(c * columns, columns), columns)
        return jnp.dot(attn, ow[:, cols], preferred_element_type=F32).astype(BF16)

    @pl.loop(0, ctx_count - 1)
    def _(k):
        c = far_first(k, ctx_count, my_c)
        p_send[c] = project(c)
        send(p_send.at[c], p_recv.at[my_c], send_sem.at[3], recv_sem.at[3], (my_g, c))

    p_recv[my_c] = project(my_c)

    experts = grp_count * EXP_GRP
    places = experts * CAPE
    expert_id = lax.broadcasted_iota(jnp.int32, (experts, req), 0)
    taken = jnp.zeros((experts, req), F32)
    table = jnp.zeros((experts, req), F32)
    for k in range(ids_ref.shape[0]):
        match = ids_ref[k : k + 1, :] == expert_id
        taken = taken + jnp.where(match, 1.0, 0.0)
        table = table + jnp.where(match, ew_ref[k : k + 1, :], 0.0)
    before = (
        lax.broadcasted_iota(jnp.int32, (req, req), 0)
        < lax.broadcasted_iota(jnp.int32, (req, req), 1)
    ).astype(F32)
    exact = functools.partial(
        jnp.dot, precision=lax.Precision.HIGHEST, preferred_element_type=F32
    )
    order = exact(taken, before)
    repeat = (
        lax.broadcasted_iota(jnp.int32, (places, experts), 0) // CAPE
        == lax.broadcasted_iota(jnp.int32, (places, experts), 1)
    ).astype(F32)
    slot = lax.rem(lax.broadcasted_iota(jnp.int32, (places, req), 0), CAPE).astype(F32)
    picked = (exact(repeat, taken) > 0.5) & (jnp.abs(exact(repeat, order) - slot) < 0.5)
    picker = picked.astype(F32).astype(BF16)
    gates = jnp.where(picked, exact(repeat, table), 0.0)
    tables = []
    for f in range(0, places, LANES):
        turn[0] = jnp.zeros((LANES, LANES), F32)
        turn[0, :, 0:req] = gates[f : f + LANES, :]
        tables.append(turn[0].T[0:req, :])
    wait_bytes(p_recv.at[pl.ds(0, ctx_count - 1)], recv_sem.at[3])
    own_cols = pl.ds(pl.multiple_of(my_c * columns, columns), columns)
    hidden = lax.fori_loop(
        0, ctx_count, lambda c, a: a + p_recv[c].astype(F32), res_ref[:, own_cols].astype(F32)
    )
    outgoing = jnp.dot(picker, hidden.astype(BF16), preferred_element_type=F32)
    for e in range(experts):
        x_send[e] = outgoing[e * CAPE : (e + 1) * CAPE, :].astype(BF16)
    parts_count = ctx_count // EXP_GRP

    def expert_of(d):
        return (d // ctx_count) * EXP_GRP + lax.rem(d, ctx_count) // parts_count

    x_recv[me] = x_send[expert_of(me)]

    @pl.loop(1, n)
    def _(k):
        d = lax.rem(me + k, n)
        send(x_send.at[expert_of(d)], x_recv.at[me], send_sem.at[4], recv_sem.at[4], dev(d))

    for i in range(6, 9):
        copies[i].wait()
    wait_bytes(x_recv.at[pl.ds(0, n - 1)], recv_sem.at[4])

    @pl.loop(0, ctx_count)
    def _(c):
        cols = pl.ds(pl.multiple_of(c * columns, columns), columns)
        for g in range(grp_count):
            xs[g * CAPE : (g + 1) * CAPE, cols] = x_recv[g * ctx_count + c].astype(F32)

    x = xs[...]
    factor = lax.rsqrt(jnp.mean(x * x, axis=1, keepdims=True) + NORM_EPSILON)
    x = (x * factor * gain_ref[...]).astype(BF16)
    units = wg.shape[0]
    step = 256 if units % 256 == 0 else units
    acts = []
    for f in range(0, units, step):
        gate = lax.dot_general(x, wg[f : f + step, :], NT, preferred_element_type=F32)
        up = lax.dot_general(x, wu[f : f + step, :], NT, preferred_element_type=F32)
        acts.append((gate / (1.0 + jnp.exp(-gate)) * up).astype(BF16))
    act = jnp.concatenate(acts, axis=1)

    @pl.loop(0, ctx_count)
    def _(k):
        c = lax.rem(my_c + k + 1, ctx_count)
        cols = pl.ds(pl.multiple_of(c * columns, columns), columns)
        y = jnp.dot(act, wd[:, cols], preferred_element_type=F32)
        for g in range(grp_count):
            y_send[g * ctx_count + c] = y[g * CAPE : (g + 1) * CAPE, :].astype(BF16)

        @pl.loop(0, grp_count)
        def _(j):
            d = lax.rem(my_g + j + 1, grp_count) * ctx_count + c

            @pl.when(d != me)
            def _():
                send(y_send.at[d], y_recv.at[me], send_sem.at[5], recv_sem.at[5], dev(d))

    y_recv[me] = y_send[me]
    wait_bytes(y_recv.at[pl.ds(0, n - 1)], recv_sem.at[5])
    for e in range(experts):
        first = e * parts_count
        y = y_recv[first].astype(F32)
        for part in range(1, parts_count):
            y = y + y_recv[first + part].astype(F32)
        ys[e * CAPE : (e + 1) * CAPE, :] = y
    out = hidden
    for f, gates in enumerate(tables):
        out = out + exact(gates, ys[f * LANES : (f + 1) * LANES, :])
    out_ref[...] = out.astype(BF16)

    wait_bytes(idx_recv.at[pl.ds(0, same_core - 1)], send_sem.at[0])
    wait_bytes(q_all.at[pl.ds(0, y_count - 1)], q_send_sem)
    wait_bytes(pk.at[0], pool_send_sem.at[0])
    wait_bytes(pv.at[0], pool_send_sem.at[1])
    for kv in range(KEY_VALUE_HEADS):
        wait_bytes(yo_send.at[kv, pl.ds(0, y_count - 1)], yo_send_sem.at[kv])
    wait_bytes(o_send.at[pl.ds(0, ctx_count - 1)], send_sem.at[1])
    wait_bytes(p_send.at[pl.ds(0, ctx_count - 1)], send_sem.at[3])
    wait_bytes(x_recv.at[pl.ds(0, n - 1)], send_sem.at[4])
    wait_bytes(y_send.at[pl.ds(0, n - 1)], send_sem.at[5])


def shards(
    queries,
    resident_key_cache,
    resident_value_cache,
    res_len,
    visual_page_pool,
    recall_holder,
    recall_slot,
    o_weight,
    residual,
    norm_gain,
    expert_ids,
    expert_weights,
    w_gate,
    w_up,
    w_down,
):
    ctx_count = lax.axis_size("ctx")
    grp_count = lax.axis_size("grp")
    n = ctx_count * grp_count
    req, q_width = queries.shape
    heads = q_width // HEAD_WIDTH
    y_count = grp_count // 2
    kv_out = q_width // KEY_VALUE_HEADS
    own_width = o_weight.shape[0]
    pages, _, page_tokens, kv_width = visual_page_pool.shape
    tokens = pages * page_tokens
    width = residual.shape[1]
    columns = width // ctx_count
    units = w_gate.shape[1]
    rows_here = resident_key_cache.shape[1]

    smem = pl.BlockSpec(memory_space=pltpu.SMEM)
    vmem = pl.BlockSpec(memory_space=pltpu.VMEM)
    hbm = pl.BlockSpec(memory_space=pl.ANY)
    return pl.pallas_call(
        functools.partial(kernel, grp_count, ctx_count, page_tokens),
        out_shape=jax.ShapeDtypeStruct((req, columns), BF16),
        in_specs=[hbm, hbm, hbm, smem, hbm, vmem, vmem, hbm, vmem, vmem, vmem, vmem, hbm, hbm, hbm],
        out_specs=vmem,
        scratch_shapes=[
            pltpu.VMEM((y_count, req, q_width), BF16),
            pltpu.VMEM((req, heads, HEAD_WIDTH), F32),
            pltpu.VMEM((req, rows_here, kv_width), BF16),
            pltpu.VMEM((req, rows_here, kv_width), BF16),
            pltpu.VMEM((2, pages, page_tokens, kv_width), BF16),
            pltpu.VMEM((2, pages, page_tokens, kv_width), BF16),
            pltpu.VMEM(o_weight.shape, BF16),
            pltpu.VMEM((units, width), BF16),
            pltpu.VMEM((units, width), BF16),
            pltpu.VMEM((units, width), BF16),
            pltpu.VMEM((2, LANES, LANES), F32),
            pltpu.VMEM((n, LANES), F32),
            pltpu.VMEM((y_count * ctx_count, 2, LANES), F32),
            pltpu.VMEM((y_count * ctx_count, 2, LANES), F32),
            pltpu.VMEM((y_count, 2 * tokens, LANES), BF16),
            pltpu.VMEM((req, heads, HEAD_WIDTH), F32),
            pltpu.VMEM((req, heads, HEAD_WIDTH), F32),
            pltpu.VMEM((KEY_VALUE_HEADS, y_count, req, kv_out + LANES), BF16),
            pltpu.VMEM((KEY_VALUE_HEADS, y_count, req, kv_out + LANES), BF16),
            pltpu.VMEM((ctx_count, req, own_width + LANES), BF16),
            pltpu.VMEM((ctx_count, req, own_width + LANES), BF16),
            pltpu.VMEM((ctx_count, req, LANES), F32),
            pltpu.VMEM((ctx_count, req, columns), BF16),
            pltpu.VMEM((ctx_count, req, columns), BF16),
            pltpu.VMEM((grp_count * EXP_GRP, CAPE, columns), BF16),
            pltpu.VMEM((n, CAPE, columns), BF16),
            pltpu.VMEM((grp_count * CAPE, width), F32),
            pltpu.VMEM((n, CAPE, columns), BF16),
            pltpu.VMEM((n, CAPE, columns), BF16),
            pltpu.VMEM((grp_count * EXP_GRP * CAPE, columns), F32),
            pltpu.SemaphoreType.DMA((9,)),
            pltpu.SemaphoreType.DMA,
            pltpu.SemaphoreType.DMA((y_count,)),
            pltpu.SemaphoreType.DMA((2,)),
            pltpu.SemaphoreType.DMA((2,)),
            pltpu.SemaphoreType.DMA((KEY_VALUE_HEADS,)),
            pltpu.SemaphoreType.DMA((KEY_VALUE_HEADS,)),
            pltpu.SemaphoreType.DMA((6,)),
            pltpu.SemaphoreType.DMA((6,)),
        ],
        compiler_params=pltpu.CompilerParams(
            collective_id=0, has_side_effects=True, vmem_limit_bytes=60 * 1024 * 1024
        ),
    )(
        queries,
        resident_key_cache,
        resident_value_cache,
        res_len,
        visual_page_pool,
        recall_holder[0],
        recall_slot[0],
        o_weight,
        residual,
        norm_gain.reshape(1, width),
        expert_ids.T,
        expert_weights.T,
        w_gate,
        w_up,
        w_down,
    )


def solution(mesh):
    placed = (
        P("grp", None),
        P("grp", "ctx", None),
        P("grp", "ctx", None),
        P("grp"),
        P(("grp", "ctx"), None, None, None),
        P("ctx", "grp", None),
        P("ctx", "grp", None),
        P("ctx", None),
        P("grp", None),
        P(),
        P("grp", None),
        P("grp", None),
        P(("grp", "ctx"), None, None),
        P(("grp", "ctx"), None, None),
        P(("grp", "ctx"), None, None),
    )
    return jax.shard_map(
        shards, mesh=mesh, in_specs=placed, out_specs=P("grp", "ctx"), check_vma=False
    )
```

```python
import functools

import jax
import jax.numpy as jnp
from jax import lax
from jax.experimental import pallas as pl
from jax.experimental.pallas import tpu as pltpu
from jax.sharding import PartitionSpec as P

KEY_VALUE_HEADS = 4
HEAD_WIDTH = 128
EXP_GRP = 8
LANES = 128
CAPE = 4
PARTS_APART = 32
EARLY = 4

VERY_NEGATIVE = -1e30
NORM_EPSILON = 1e-06
LOG2E = 1.4426950408889634
SCALE = HEAD_WIDTH ** (-0.5)

NT = (((1,), (1,)), ((), ()))
F32 = jnp.float32
BF16 = jnp.bfloat16


def wait_bytes(ref, sem):
    pltpu.make_async_copy(ref, ref, sem).wait()


def kernel(
    grp_count,
    ctx_count,
    page_tokens,
    q_hbm,
    kc_hbm,
    vc_hbm,
    rl_ref,
    pool_hbm,
    holder_ref,
    slot_ref,
    ow_hbm,
    res_ref,
    gain_ref,
    ids_ref,
    ew_ref,
    wg_hbm,
    wu_hbm,
    wd_hbm,
    out_ref,
    q_all,
    qt,
    kc,
    vc,
    pk,
    pv,
    ow,
    wg,
    wu,
    wd,
    turn,
    named,
    msg_ref,
    idx_recv,
    bias,
    o_res,
    l_res,
    yo_send,
    yo_recv,
    o_send,
    o_recv,
    mix_w,
    p_send,
    p_recv,
    x_send,
    x_recv,
    y_send,
    y_recv,
    ys,
    local_sem,
    q_send_sem,
    q_recv_sem,
    pool_send_sem,
    pool_recv_sem,
    yo_send_sem,
    yo_recv_sem,
    x_recv_sem,
    send_sem,
    recv_sem,
):
    n = grp_count * ctx_count
    my_g = lax.axis_index("grp")
    my_c = lax.axis_index("ctx")
    me = my_g * ctx_count + my_c
    y_count = grp_count // 2
    my_y = my_g // 2
    my_core = lax.rem(my_g, 2)
    pair = (my_g + 1 - 2 * my_core, my_c)
    req = q_all.shape[1]
    heads = qt.shape[1]
    per_kv = heads // KEY_VALUE_HEADS
    kv_out = per_kv * HEAD_WIDTH
    own_width = o_send.shape[2] - LANES
    heads_each = own_width // HEAD_WIDTH
    c_per_kv = per_kv // heads_each
    page_count = pk.shape[1]
    tokens = page_count * page_tokens
    columns = p_send.shape[2]
    same_core = y_count * ctx_count
    mine = my_y * ctx_count + my_c

    def dev(d):
        return (d // ctx_count, lax.rem(d, ctx_count))

    def far_first(k, count, at):
        above, below = count - 1 - at, at
        most, least = jnp.maximum(above, below), jnp.minimum(above, below)
        lead = most - least
        j = jnp.maximum(k - lead, 0)
        side = jnp.where(above >= below, 1, -1) * (1 - 2 * lax.rem(j, 2))
        return at + side * jnp.where(k < lead, most - k, least - j // 2)

    early, late = pl.ds(0, EARLY), pl.ds(EARLY, req - EARLY)
    loads = [
        (q_hbm, q_all.at[my_y]),
        (kc_hbm.at[early], kc.at[early]),
        (vc_hbm.at[early], vc.at[early]),
        (kc_hbm.at[late], kc.at[late]),
        (vc_hbm.at[late], vc.at[late]),
        (pool_hbm.at[:, 0], pk.at[my_core]),
        (pool_hbm.at[:, 1], pv.at[my_core]),
        (ow_hbm, ow),
        (wg_hbm.at[0], wg),
        (wu_hbm.at[0], wu),
        (wd_hbm.at[0], wd),
    ]
    copies = [pltpu.make_async_copy(s, d, local_sem.at[i]) for i, (s, d) in enumerate(loads)]
    for copy in copies[:7]:
        copy.start()

    barrier = pltpu.get_barrier_semaphore()

    def greet(g, c):
        pl.semaphore_signal(
            barrier, inc=1, device_id=(g, c), device_id_type=pl.DeviceIdType.MESH
        )

    @pl.loop(0, ctx_count - 1)
    def _(k):
        for g in range(grp_count):
            greet(g, far_first(k, ctx_count, my_c))

    for k in range(1, grp_count):
        greet(lax.rem(my_g + k, grp_count), my_c)

    lists = holder_ref.shape[1]
    for i, ref in enumerate((holder_ref, slot_ref)):
        turn[i] = jnp.zeros((LANES, LANES), F32)
        for r in range(3):
            turn[i, r * req : (r + 1) * req, 0:lists] = ref[...].astype(F32)
    holder_t = turn[0].T
    slot_t = turn[1].T
    holder_id = lax.broadcasted_iota(jnp.int32, (n, LANES), 0).astype(F32)
    table = jnp.zeros((n, LANES), F32)
    for j in range(lists):
        table = table + jnp.where(
            holder_t[j : j + 1, :] == holder_id, slot_t[j : j + 1, :] + 1.0, 0.0
        )
    named[...] = table

    @pl.loop(0, same_core)
    def _(i):
        first = (i // ctx_count) * 2 * ctx_count + lax.rem(i, ctx_count)
        msg_ref[i, 0:1, :] = named[pl.ds(first, 1), :]
        msg_ref[i, 1:2, :] = named[pl.ds(first + ctx_count, 1), :]

    rows_here = kc.shape[1]

    def resident(t, carry):
        pos = my_c * rows_here + lax.broadcasted_iota(jnp.int32, (heads, rows_here), 1)
        ok = pos < rl_ref[t]
        s = jnp.concatenate(
            [
                lax.dot_general(
                    qt[t, k * per_kv : (k + 1) * per_kv, :].astype(BF16),
                    kc[t, :, k * HEAD_WIDTH : (k + 1) * HEAD_WIDTH],
                    NT,
                    preferred_element_type=F32,
                )
                for k in range(KEY_VALUE_HEADS)
            ],
            axis=0,
        )
        s = jnp.where(ok, s, VERY_NEGATIVE)
        m = jnp.max(s, axis=1, keepdims=True)
        p = jnp.exp2((s - m) * (SCALE * LOG2E))
        p = jnp.where(ok, p, 0.0)
        total = jnp.maximum(jnp.sum(p, axis=1, keepdims=True), 1e-30)
        pb = p.astype(BF16)
        o = jnp.concatenate(
            [
                jnp.dot(
                    pb[k * per_kv : (k + 1) * per_kv, :],
                    vc[t, :, k * HEAD_WIDTH : (k + 1) * HEAD_WIDTH],
                    preferred_element_type=F32,
                )
                for k in range(KEY_VALUE_HEADS)
            ],
            axis=0,
        )
        o_res[t] = o / total
        lse = m * (SCALE * LOG2E) + jnp.log(total) * LOG2E
        l_res[t] = jnp.broadcast_to(lse, (heads, LANES))
        return carry

    copies[0].wait()
    for h in range(heads):
        qt[:, h, :] = q_all[my_y, :, h * HEAD_WIDTH : (h + 1) * HEAD_WIDTH].astype(F32)
    copies[1].wait()
    copies[2].wait()
    lax.fori_loop(0, EARLY, resident, 0, unroll=4)

    pl.semaphore_wait(barrier, n - 1)

    def send(src, dst, s_sem, r_sem, target):
        pltpu.make_async_remote_copy(
            src_ref=src,
            dst_ref=dst,
            send_sem=s_sem,
            recv_sem=r_sem,
            device_id=target,
            device_id_type=pl.DeviceIdType.MESH,
        ).start()

    for i in range(2):
        send(
            pool_hbm.at[:, i],
            (pk, pv)[i].at[my_core],
            pool_send_sem.at[i],
            pool_recv_sem.at[i],
            pair,
        )

    def send_lists(y, c):
        send(
            msg_ref.at[y * ctx_count + c],
            idx_recv.at[mine],
            send_sem.at[0],
            recv_sem.at[0],
            (y * 2 + my_core, c),
        )

    @pl.loop(0, ctx_count - 1)
    def _(k):
        for y in range(y_count):
            send_lists(y, far_first(k, ctx_count, my_c))

    for k in range(1, y_count):
        send_lists(lax.rem(my_y + k, y_count), my_c)

    for k in range(1, y_count):
        y = lax.rem(my_y + k, y_count)
        for i in range(KEY_VALUE_HEADS):
            kv = far_first(i, KEY_VALUE_HEADS, my_c // c_per_kv)
            cols = pl.ds(pl.multiple_of(kv * kv_out, kv_out), kv_out)
            send(
                q_hbm.at[:, cols],
                q_all.at[my_y, :, cols],
                q_send_sem,
                q_recv_sem.at[my_y, kv],
                (y * 2 + my_core, my_c),
            )

    for copy in copies[7:]:
        copy.start()

    idx_recv[mine] = msg_ref[mine]
    copies[3].wait()
    copies[4].wait()
    lax.fori_loop(EARLY, req, resident, 0, unroll=4)

    wait_bytes(idx_recv.at[pl.ds(0, same_core - 1)], recv_sem.at[0])
    lane = lax.broadcasted_iota(jnp.int32, (page_count, LANES), 1)
    page_id = (lax.broadcasted_iota(jnp.int32, (page_count, LANES), 0) + 1).astype(F32)
    spread = (
        lax.broadcasted_iota(jnp.int32, (tokens, page_count), 0) // page_tokens
        == lax.broadcasted_iota(jnp.int32, (tokens, page_count), 1)
    ).astype(F32).astype(BF16)

    @pl.loop(0, y_count)
    def _(y):
        for core in range(2):
            def add(c, count):
                row = idx_recv[y * ctx_count + c, core : core + 1, :]
                return count + (jnp.broadcast_to(row, page_id.shape) == page_id).astype(F32)

            count = lax.fori_loop(0, ctx_count, add, jnp.zeros((page_count, LANES), F32), unroll=8)
            level = jnp.where(
                count > 0.0, jnp.log(jnp.maximum(count, 1.0)) * (1.0 / SCALE), VERY_NEGATIVE
            )
            hi = level.astype(BF16).astype(F32)
            rest = jnp.where(count > 0.0, level - hi, 0.0)
            mid = rest.astype(BF16).astype(F32)
            low = rest - mid
            part = jnp.where(lane < req, hi, jnp.where(lane < 2 * req, mid, low))
            part = jnp.where(lane < 3 * req, part, 0.0).astype(BF16)
            bias[y, core * tokens : (core + 1) * tokens, :] = jnp.dot(
                spread, part, preferred_element_type=F32
            ).astype(BF16)

    copies[5].wait()
    copies[6].wait()
    wait_bytes(pk.at[0], pool_recv_sem.at[0])
    wait_bytes(pv.at[0], pool_recv_sem.at[1])
    rows = per_kv * req
    row_t = lax.rem(lax.broadcasted_iota(jnp.int32, (rows, LANES), 0), req)
    row_lane = lax.broadcasted_iota(jnp.int32, (rows, LANES), 1)
    chooser = (
        ((lax.rem(row_lane, req) == row_t) & (row_lane < 3 * req)).astype(F32).astype(BF16)
    )
    st_lane = lax.broadcasted_iota(jnp.int32, (req, LANES), 1)

    def encode(stat):
        hi = stat.astype(BF16).astype(F32)
        rest = stat - hi
        mid = rest.astype(BF16).astype(F32)
        low = rest - mid
        return (hi + pltpu.roll(mid, PARTS_APART, 1) + pltpu.roll(low, 2 * PARTS_APART, 1)).astype(BF16)

    def decode(block):
        x = block.astype(F32)
        return (
            x + pltpu.roll(x, LANES - PARTS_APART, 1) + pltpu.roll(x, LANES - 2 * PARTS_APART, 1)
        )

    def pool_scores(y, kv):
        qk = jnp.concatenate(
            [
                q_all[
                    y,
                    :,
                    pl.ds(pl.multiple_of((kv * per_kv + h) * HEAD_WIDTH, HEAD_WIDTH), HEAD_WIDTH),
                ]
                for h in range(per_kv)
            ],
            axis=0,
        )
        kv_cols = pl.ds(pl.multiple_of(kv * HEAD_WIDTH, HEAD_WIDTH), HEAD_WIDTH)
        qa = jnp.concatenate([qk, chooser], axis=1)
        ka = jnp.concatenate(
            [pk[:, :, :, kv_cols].reshape(2 * tokens, HEAD_WIDTH), bias[y]], axis=1
        )
        s = lax.dot_general(qa, ka, NT, preferred_element_type=F32)
        return s, jnp.max(s, axis=1, keepdims=True)

    def pool_values(kv, s, m):
        kv_cols = pl.ds(pl.multiple_of(kv * HEAD_WIDTH, HEAD_WIDTH), HEAD_WIDTH)
        p = jnp.exp2((s - m) * (SCALE * LOG2E)).astype(BF16)
        va = jnp.concatenate(
            [
                pv[:, :, :, kv_cols].reshape(2 * tokens, HEAD_WIDTH),
                jnp.ones((2 * tokens, LANES), BF16),
            ],
            axis=1,
        )
        o = jnp.dot(p, va, preferred_element_type=F32)
        top = jnp.broadcast_to(m * (SCALE * LOG2E), (rows, LANES))
        return o[:, :HEAD_WIDTH], o[:, HEAD_WIDTH:], top

    def pool_parts(y, kvs):
        scores = [pool_scores(y, kv) for kv in kvs]
        return [pool_values(kv, *x) for kv, x in zip(kvs, scores)]

    def of_head(x, h):
        return x[h * req : (h + 1) * req, :]

    my_kv = my_c // c_per_kv

    @pl.loop(1, y_count)
    def _(k):
        y = lax.rem(my_y + k, y_count)
        for first in range(0, KEY_VALUE_HEADS, 2):
            kvs = [far_first(first + i, KEY_VALUE_HEADS, my_kv) for i in range(2)]
            for kv in kvs:
                wait_bytes(q_all.at[y, :, pl.ds(0, kv_out)], q_recv_sem.at[y, kv])
            for kv, (o, total, top) in zip(kvs, pool_parts(y, kvs)):
                o = o / total
                lse = top + jnp.log(total) * LOG2E
                stat = jnp.zeros((req, LANES), F32)
                for h in range(per_kv):
                    yo_send[kv, y, :, h * HEAD_WIDTH : (h + 1) * HEAD_WIDTH] = of_head(o, h).astype(BF16)
                    stat = jnp.where(st_lane == h, of_head(lse, h), stat)
                yo_send[kv, y, :, kv_out:] = encode(stat)
            for kv in kvs:
                send(
                    yo_send.at[kv, y],
                    yo_recv.at[kv, my_y],
                    yo_send_sem.at[kv],
                    yo_recv_sem.at[kv],
                    (y * 2 + my_core, my_c),
                )

    for first in range(0, KEY_VALUE_HEADS, 2):
        kvs = [far_first(first + i, KEY_VALUE_HEADS, my_kv) for i in range(2)]
        parts = pool_parts(my_y, kvs)
        for kv in kvs:
            wait_bytes(yo_recv.at[kv, pl.ds(0, y_count - 1)], yo_recv_sem.at[kv])
        for i, (kv, (o, total, top)) in enumerate(zip(kvs, parts)):
            others = []
            for k in range(1, y_count):
                y = lax.rem(my_y + k, y_count)
                others.append((y, decode(yo_recv[kv, y, :, kv_out:])))
            for b in range(c_per_kv):
                c = kv * c_per_kv + b
                stat = jnp.zeros((req, LANES), F32)
                for j in range(heads_each):
                    h = b * heads_each + j
                    terms = [
                        (of_head(top, h), of_head(total, h), of_head(o, h)),
                        (l_res[:, kv * per_kv + h, :], None, o_res[:, kv * per_kv + h, :]),
                    ]
                    for y, l_y in others:
                        o_y = yo_recv[kv, y, :, h * HEAD_WIDTH : (h + 1) * HEAD_WIDTH].astype(F32)
                        terms.append((jnp.broadcast_to(l_y[:, h : h + 1], (req, LANES)), None, o_y))
                    best = functools.reduce(jnp.maximum, [t[0] for t in terms])
                    weights = [jnp.exp2(t[0] - best) for t in terms]
                    mass = sum(w if t[1] is None else w * t[1] for w, t in zip(weights, terms))
                    o_h = sum(w * t[2] for w, t in zip(weights, terms)) / mass
                    l_h = best + jnp.log(mass) * LOG2E
                    o_send[c, :, j * HEAD_WIDTH : (j + 1) * HEAD_WIDTH] = o_h.astype(BF16)
                    stat = jnp.where(st_lane == j, l_h, stat)
                o_send[c, :, own_width:] = encode(stat)
            last = first + i == KEY_VALUE_HEADS - 1
            for b in range(1 if last else 0, c_per_kv):
                c = kv * c_per_kv + (lax.rem(my_c + b, c_per_kv) if last else b)
                send(o_send.at[c], o_recv.at[my_c], send_sem.at[1], recv_sem.at[1], (my_g, c))

    o_recv[my_c] = o_send[my_c]
    wait_bytes(o_recv.at[pl.ds(0, ctx_count - 1)], recv_sem.at[1])

    def highest(i, top):
        level = decode(o_recv[i, :, own_width:])
        mix_w[i] = level
        return jnp.maximum(top, level)

    top = lax.fori_loop(0, ctx_count, highest, jnp.full((req, LANES), -3e38, F32), unroll=8)

    def weigh(i, total):
        w = jnp.exp2(mix_w[i] - top)
        mix_w[i] = w
        return total + w

    total = lax.fori_loop(0, ctx_count, weigh, jnp.zeros((req, LANES), F32), unroll=8)
    inverse = 1.0 / total

    def join(i, acc):
        w = mix_w[i] * inverse
        return tuple(
            acc[j]
            + w[:, j : j + 1] * o_recv[i, :, j * HEAD_WIDTH : (j + 1) * HEAD_WIDTH].astype(F32)
            for j in range(heads_each)
        )

    acc = lax.fori_loop(
        0,
        ctx_count,
        join,
        tuple(jnp.zeros((req, HEAD_WIDTH), F32) for _ in range(heads_each)),
        unroll=8,
    )
    attn = jnp.concatenate([a.astype(BF16) for a in acc], axis=1)

    copies[7].wait()

    def project(c):
        cols = pl.ds(pl.multiple_of(c * columns, columns), columns)
        return jnp.dot(attn, ow[:, cols], preferred_element_type=F32).astype(BF16)

    @pl.loop(0, ctx_count - 1)
    def _(k):
        c = far_first(k, ctx_count, my_c)
        p_send[c] = project(c)
        send(p_send.at[c], p_recv.at[my_c], send_sem.at[3], recv_sem.at[3], (my_g, c))

    p_recv[my_c] = project(my_c)

    experts = grp_count * EXP_GRP
    places = experts * CAPE
    expert_id = lax.broadcasted_iota(jnp.int32, (experts, req), 0)
    taken = jnp.zeros((experts, req), F32)
    table = jnp.zeros((experts, req), F32)
    for k in range(ids_ref.shape[0]):
        match = ids_ref[k : k + 1, :] == expert_id
        taken = taken + jnp.where(match, 1.0, 0.0)
        table = table + jnp.where(match, ew_ref[k : k + 1, :], 0.0)
    before = (
        lax.broadcasted_iota(jnp.int32, (req, req), 0)
        < lax.broadcasted_iota(jnp.int32, (req, req), 1)
    ).astype(F32)
    exact = functools.partial(
        jnp.dot, precision=lax.Precision.HIGHEST, preferred_element_type=F32
    )
    order = exact(taken, before)
    repeat = (
        lax.broadcasted_iota(jnp.int32, (places, experts), 0) // CAPE
        == lax.broadcasted_iota(jnp.int32, (places, experts), 1)
    ).astype(F32)
    slot = lax.rem(lax.broadcasted_iota(jnp.int32, (places, req), 0), CAPE).astype(F32)
    picked = (exact(repeat, taken) > 0.5) & (jnp.abs(exact(repeat, order) - slot) < 0.5)
    picker = picked.astype(F32).astype(BF16)
    gates = jnp.where(picked, exact(repeat, table), 0.0)
    tables = []
    for f in range(0, places, LANES):
        turn[0] = jnp.zeros((LANES, LANES), F32)
        turn[0, :, 0:req] = gates[f : f + LANES, :]
        tables.append(turn[0].T[0:req, :])
    wait_bytes(p_recv.at[pl.ds(0, ctx_count - 1)], recv_sem.at[3])
    own_cols = pl.ds(pl.multiple_of(my_c * columns, columns), columns)
    hidden = lax.fori_loop(
        0, ctx_count, lambda c, a: a + p_recv[c].astype(F32), res_ref[:, own_cols].astype(F32)
    )
    outgoing = jnp.dot(picker, hidden.astype(BF16), preferred_element_type=F32)
    for e in range(experts):
        x_send[e] = outgoing[e * CAPE : (e + 1) * CAPE, :].astype(BF16)
    parts_count = ctx_count // EXP_GRP

    def expert_of(d):
        return (d // ctx_count) * EXP_GRP + lax.rem(d, ctx_count) // parts_count

    def dispatch(g, c):
        send(
            x_send.at[expert_of(g * ctx_count + c)],
            x_recv.at[my_c, my_g],
            send_sem.at[4],
            x_recv_sem.at[my_c],
            (g, c),
        )

    @pl.loop(0, ctx_count - 1)
    def _(k):
        for g in range(grp_count):
            dispatch(g, far_first(k, ctx_count, my_c))

    for k in range(1, grp_count):
        dispatch(lax.rem(my_g + k, grp_count), my_c)
    x_recv[my_c, my_g] = x_send[expert_of(me)]

    for i in range(8, 10):
        copies[i].wait()
    units = wg.shape[0]
    width = wg.shape[1]
    slots = grp_count * CAPE

    def gate_up(c, carry):
        squares, gate, up = carry
        cols = pl.ds(pl.multiple_of(c * columns, columns), columns)
        x = jnp.concatenate([x_recv[c, g].astype(F32) for g in range(grp_count)], axis=0)
        squares = squares + jnp.sum(x * x, axis=1, keepdims=True)
        x = (x * gain_ref[:, cols]).astype(BF16)
        gate = gate + lax.dot_general(x, wg[:, cols], NT, preferred_element_type=F32)
        up = up + lax.dot_general(x, wu[:, cols], NT, preferred_element_type=F32)
        return squares, gate, up

    def arrived(k, carry):
        c = far_first(ctx_count - 1 - k, ctx_count, my_c)
        wait_bytes(x_recv.at[c], x_recv_sem.at[c])
        return gate_up(c, carry)

    wait_bytes(x_recv.at[my_c, pl.ds(0, grp_count - 1)], x_recv_sem.at[my_c])
    nothing = jnp.zeros((slots, units), F32)
    carry = gate_up(my_c, (jnp.zeros((slots, 1), F32), nothing, nothing))
    squares, gate, up = lax.fori_loop(1, ctx_count, arrived, carry)
    factor = lax.rsqrt(squares * (1.0 / width) + NORM_EPSILON)
    gate = gate * factor
    up = up * factor
    act = (gate / (1.0 + jnp.exp(-gate)) * up).astype(BF16)
    copies[10].wait()

    def down(c):
        cols = pl.ds(pl.multiple_of(c * columns, columns), columns)
        y = jnp.dot(act, wd[:, cols], preferred_element_type=F32)
        for g in range(grp_count):
            y_send[g * ctx_count + c] = y[g * CAPE : (g + 1) * CAPE, :].astype(BF16)

    def give_back(g, c):
        send(y_send.at[g * ctx_count + c], y_recv.at[me], send_sem.at[5], recv_sem.at[5], (g, c))

    @pl.loop(0, ctx_count - 1)
    def _(k):
        c = far_first(k, ctx_count, my_c)
        down(c)
        for g in range(grp_count):
            give_back(g, c)

    down(my_c)
    for k in range(1, grp_count):
        give_back(lax.rem(my_g + k, grp_count), my_c)
    y_recv[me] = y_send[me]
    wait_bytes(y_recv.at[pl.ds(0, n - 1)], recv_sem.at[5])
    for e in range(experts):
        first = e * parts_count
        y = y_recv[first].astype(F32)
        for part in range(1, parts_count):
            y = y + y_recv[first + part].astype(F32)
        ys[e * CAPE : (e + 1) * CAPE, :] = y
    out = hidden
    for f, gates in enumerate(tables):
        out = out + exact(gates, ys[f * LANES : (f + 1) * LANES, :])
    out_ref[...] = out.astype(BF16)

    wait_bytes(idx_recv.at[pl.ds(0, same_core - 1)], send_sem.at[0])
    wait_bytes(q_all.at[pl.ds(0, y_count - 1)], q_send_sem)
    wait_bytes(pk.at[0], pool_send_sem.at[0])
    wait_bytes(pv.at[0], pool_send_sem.at[1])
    for kv in range(KEY_VALUE_HEADS):
        wait_bytes(yo_send.at[kv, pl.ds(0, y_count - 1)], yo_send_sem.at[kv])
    wait_bytes(o_send.at[pl.ds(0, ctx_count - 1)], send_sem.at[1])
    wait_bytes(p_send.at[pl.ds(0, ctx_count - 1)], send_sem.at[3])
    wait_bytes(y_recv.at[pl.ds(0, n - 1)], send_sem.at[4])
    wait_bytes(y_send.at[pl.ds(0, n - 1)], send_sem.at[5])


def shards(
    queries,
    resident_key_cache,
    resident_value_cache,
    res_len,
    visual_page_pool,
    recall_holder,
    recall_slot,
    o_weight,
    residual,
    norm_gain,
    expert_ids,
    expert_weights,
    w_gate,
    w_up,
    w_down,
):
    ctx_count = lax.axis_size("ctx")
    grp_count = lax.axis_size("grp")
    n = ctx_count * grp_count
    req, q_width = queries.shape
    heads = q_width // HEAD_WIDTH
    y_count = grp_count // 2
    kv_out = q_width // KEY_VALUE_HEADS
    own_width = o_weight.shape[0]
    pages, _, page_tokens, kv_width = visual_page_pool.shape
    tokens = pages * page_tokens
    width = residual.shape[1]
    columns = width // ctx_count
    units = w_gate.shape[1]
    rows_here = resident_key_cache.shape[1]

    smem = pl.BlockSpec(memory_space=pltpu.SMEM)
    vmem = pl.BlockSpec(memory_space=pltpu.VMEM)
    hbm = pl.BlockSpec(memory_space=pl.ANY)
    return pl.pallas_call(
        functools.partial(kernel, grp_count, ctx_count, page_tokens),
        out_shape=jax.ShapeDtypeStruct((req, columns), BF16),
        in_specs=[hbm, hbm, hbm, smem, hbm, vmem, vmem, hbm, vmem, vmem, vmem, vmem, hbm, hbm, hbm],
        out_specs=vmem,
        scratch_shapes=[
            pltpu.VMEM((y_count, req, q_width), BF16),
            pltpu.VMEM((req, heads, HEAD_WIDTH), F32),
            pltpu.VMEM((req, rows_here, kv_width), BF16),
            pltpu.VMEM((req, rows_here, kv_width), BF16),
            pltpu.VMEM((2, pages, page_tokens, kv_width), BF16),
            pltpu.VMEM((2, pages, page_tokens, kv_width), BF16),
            pltpu.VMEM(o_weight.shape, BF16),
            pltpu.VMEM((units, width), BF16),
            pltpu.VMEM((units, width), BF16),
            pltpu.VMEM((units, width), BF16),
            pltpu.VMEM((2, LANES, LANES), F32),
            pltpu.VMEM((n, LANES), F32),
            pltpu.VMEM((y_count * ctx_count, 2, LANES), F32),
            pltpu.VMEM((y_count * ctx_count, 2, LANES), F32),
            pltpu.VMEM((y_count, 2 * tokens, LANES), BF16),
            pltpu.VMEM((req, heads, HEAD_WIDTH), F32),
            pltpu.VMEM((req, heads, HEAD_WIDTH), F32),
            pltpu.VMEM((KEY_VALUE_HEADS, y_count, req, kv_out + LANES), BF16),
            pltpu.VMEM((KEY_VALUE_HEADS, y_count, req, kv_out + LANES), BF16),
            pltpu.VMEM((ctx_count, req, own_width + LANES), BF16),
            pltpu.VMEM((ctx_count, req, own_width + LANES), BF16),
            pltpu.VMEM((ctx_count, req, LANES), F32),
            pltpu.VMEM((ctx_count, req, columns), BF16),
            pltpu.VMEM((ctx_count, req, columns), BF16),
            pltpu.VMEM((grp_count * EXP_GRP, CAPE, columns), BF16),
            pltpu.VMEM((ctx_count, grp_count, CAPE, columns), BF16),
            pltpu.VMEM((n, CAPE, columns), BF16),
            pltpu.VMEM((n, CAPE, columns), BF16),
            pltpu.VMEM((grp_count * EXP_GRP * CAPE, columns), F32),
            pltpu.SemaphoreType.DMA((11,)),
            pltpu.SemaphoreType.DMA,
            pltpu.SemaphoreType.DMA((y_count, KEY_VALUE_HEADS)),
            pltpu.SemaphoreType.DMA((2,)),
            pltpu.SemaphoreType.DMA((2,)),
            pltpu.SemaphoreType.DMA((KEY_VALUE_HEADS,)),
            pltpu.SemaphoreType.DMA((KEY_VALUE_HEADS,)),
            pltpu.SemaphoreType.DMA((ctx_count,)),
            pltpu.SemaphoreType.DMA((6,)),
            pltpu.SemaphoreType.DMA((6,)),
        ],
        compiler_params=pltpu.CompilerParams(
            collective_id=0, has_side_effects=True, vmem_limit_bytes=60 * 1024 * 1024
        ),
    )(
        queries,
        resident_key_cache,
        resident_value_cache,
        res_len,
        visual_page_pool,
        recall_holder[0],
        recall_slot[0],
        o_weight,
        residual,
        norm_gain.reshape(1, width),
        expert_ids.T,
        expert_weights.T,
        w_gate,
        w_up,
        w_down,
    )


def solution(mesh):
    placed = (
        P("grp", None),
        P("grp", "ctx", None),
        P("grp", "ctx", None),
        P("grp"),
        P(("grp", "ctx"), None, None, None),
        P("ctx", "grp", None),
        P("ctx", "grp", None),
        P("ctx", None),
        P("grp", None),
        P(),
        P("grp", None),
        P("grp", None),
        P(("grp", "ctx"), None, None),
        P(("grp", "ctx"), None, None),
        P(("grp", "ctx"), None, None),
    )
    return jax.shard_map(
        shards, mesh=mesh, in_specs=placed, out_specs=P("grp", "ctx"), check_vma=False
    )
```

```python
import functools

import jax
import jax.numpy as jnp
from jax import lax
from jax.experimental import pallas as pl
from jax.experimental.pallas import tpu as pltpu
from jax.sharding import PartitionSpec as P

KEY_VALUE_HEADS = 4
HEAD_WIDTH = 128
EXP_GRP = 8
LANES = 128
CAPE = 4
PARTS_APART = 32
EARLY = 4

VERY_NEGATIVE = -1e30
NORM_EPSILON = 1e-06
LOG2E = 1.4426950408889634
SCALE = HEAD_WIDTH ** (-0.5)

NT = (((1,), (1,)), ((), ()))
F32 = jnp.float32
BF16 = jnp.bfloat16


def wait_bytes(ref, sem):
    pltpu.make_async_copy(ref, ref, sem).wait()


def kernel(
    grp_count,
    ctx_count,
    page_tokens,
    q_hbm,
    kc_hbm,
    vc_hbm,
    rl_hbm,
    pool_hbm,
    holder_hbm,
    slot_hbm,
    ow_hbm,
    res_hbm,
    gain_hbm,
    ids_hbm,
    ew_hbm,
    wg_hbm,
    wu_hbm,
    wd_hbm,
    out_ref,
    rl_ref,
    holder_ref,
    slot_ref,
    res_ref,
    gain_ref,
    ids_ref,
    ew_ref,
    q_all,
    qt,
    kc,
    vc,
    pk,
    pv,
    ow,
    wg,
    wu,
    wd,
    turn,
    named,
    msg_ref,
    idx_recv,
    bias,
    o_res,
    l_res,
    yo_send,
    yo_recv,
    o_send,
    o_recv,
    mix_w,
    p_send,
    p_recv,
    x_send,
    x_recv,
    y_send,
    y_recv,
    ys,
    local_sem,
    small_sem,
    q_send_sem,
    q_recv_sem,
    pool_send_sem,
    pool_recv_sem,
    yo_send_sem,
    yo_recv_sem,
    x_recv_sem,
    send_sem,
    recv_sem,
):
    n = grp_count * ctx_count
    my_g = lax.axis_index("grp")
    my_c = lax.axis_index("ctx")
    me = my_g * ctx_count + my_c
    y_count = grp_count // 2
    my_y = my_g // 2
    my_core = lax.rem(my_g, 2)
    pair = (my_g + 1 - 2 * my_core, my_c)
    req = q_all.shape[1]
    heads = qt.shape[1]
    per_kv = heads // KEY_VALUE_HEADS
    kv_out = per_kv * HEAD_WIDTH
    own_width = o_send.shape[2] - LANES
    heads_each = own_width // HEAD_WIDTH
    c_per_kv = per_kv // heads_each
    page_count = pk.shape[1]
    tokens = page_count * page_tokens
    columns = p_send.shape[2]
    same_core = y_count * ctx_count
    mine = my_y * ctx_count + my_c

    def dev(d):
        return (d // ctx_count, lax.rem(d, ctx_count))

    def far_first(k, count, at):
        above, below = count - 1 - at, at
        most, least = jnp.maximum(above, below), jnp.minimum(above, below)
        lead = most - least
        j = jnp.maximum(k - lead, 0)
        side = jnp.where(above >= below, 1, -1) * (1 - 2 * lax.rem(j, 2))
        return at + side * jnp.where(k < lead, most - k, least - j // 2)

    early, late = pl.ds(0, EARLY), pl.ds(EARLY, req - EARLY)
    loads = [
        (q_hbm, q_all.at[my_y]),
        (kc_hbm.at[early], kc.at[early]),
        (vc_hbm.at[early], vc.at[early]),
        (kc_hbm.at[late], kc.at[late]),
        (vc_hbm.at[late], vc.at[late]),
        (pool_hbm.at[:, 0], pk.at[my_core]),
        (pool_hbm.at[:, 1], pv.at[my_core]),
        (ow_hbm, ow),
        (wg_hbm.at[0], wg),
        (wu_hbm.at[0], wu),
        (wd_hbm.at[0], wd),
    ]
    copies = [pltpu.make_async_copy(s, d, local_sem.at[i]) for i, (s, d) in enumerate(loads)]
    own_cols = pl.ds(pl.multiple_of(my_c * columns, columns), columns)
    small_loads = [
        (holder_hbm, holder_ref),
        (slot_hbm, slot_ref),
        (rl_hbm, rl_ref),
        (ids_hbm, ids_ref),
        (ew_hbm, ew_ref),
        (res_hbm.at[:, own_cols], res_ref),
        (gain_hbm, gain_ref),
    ]
    small = [pltpu.make_async_copy(s, d, small_sem.at[i]) for i, (s, d) in enumerate(small_loads)]
    for copy in small[:2] + copies[:3] + small[2:] + copies[3:7]:
        copy.start()

    barrier = pltpu.get_barrier_semaphore()

    def greet(g, c):
        pl.semaphore_signal(
            barrier, inc=1, device_id=(g, c), device_id_type=pl.DeviceIdType.MESH
        )

    @pl.loop(0, ctx_count - 1)
    def _(k):
        for g in range(grp_count):
            greet(g, far_first(k, ctx_count, my_c))

    for k in range(1, grp_count):
        greet(lax.rem(my_g + k, grp_count), my_c)

    small[0].wait()
    small[1].wait()
    lists = holder_ref.shape[1]
    for i, ref in enumerate((holder_ref, slot_ref)):
        turn[i] = jnp.zeros((LANES, LANES), F32)
        for r in range(3):
            turn[i, r * req : (r + 1) * req, 0:lists] = ref[...].astype(F32)
    holder_t = turn[0].T
    slot_t = turn[1].T
    holder_id = lax.broadcasted_iota(jnp.int32, (n, LANES), 0).astype(F32)
    table = jnp.zeros((n, LANES), F32)
    for j in range(lists):
        table = table + jnp.where(
            holder_t[j : j + 1, :] == holder_id, slot_t[j : j + 1, :] + 1.0, 0.0
        )
    named[...] = table

    @pl.loop(0, same_core)
    def _(i):
        first = (i // ctx_count) * 2 * ctx_count + lax.rem(i, ctx_count)
        msg_ref[i, 0:1, :] = named[pl.ds(first, 1), :]
        msg_ref[i, 1:2, :] = named[pl.ds(first + ctx_count, 1), :]

    rows_here = kc.shape[1]

    def resident(t, carry):
        pos = my_c * rows_here + lax.broadcasted_iota(jnp.int32, (heads, rows_here), 1)
        ok = pos < rl_ref[t]
        s = jnp.concatenate(
            [
                lax.dot_general(
                    qt[t, k * per_kv : (k + 1) * per_kv, :].astype(BF16),
                    kc[t, :, k * HEAD_WIDTH : (k + 1) * HEAD_WIDTH],
                    NT,
                    preferred_element_type=F32,
                )
                for k in range(KEY_VALUE_HEADS)
            ],
            axis=0,
        )
        s = jnp.where(ok, s, VERY_NEGATIVE)
        m = jnp.max(s, axis=1, keepdims=True)
        p = jnp.exp2((s - m) * (SCALE * LOG2E))
        p = jnp.where(ok, p, 0.0)
        total = jnp.maximum(jnp.sum(p, axis=1, keepdims=True), 1e-30)
        pb = p.astype(BF16)
        o = jnp.concatenate(
            [
                jnp.dot(
                    pb[k * per_kv : (k + 1) * per_kv, :],
                    vc[t, :, k * HEAD_WIDTH : (k + 1) * HEAD_WIDTH],
                    preferred_element_type=F32,
                )
                for k in range(KEY_VALUE_HEADS)
            ],
            axis=0,
        )
        o_res[t] = o / total
        lse = m * (SCALE * LOG2E) + jnp.log(total) * LOG2E
        l_res[t] = jnp.broadcast_to(lse, (heads, LANES))
        return carry

    copies[0].wait()
    for h in range(heads):
        qt[:, h, :] = q_all[my_y, :, h * HEAD_WIDTH : (h + 1) * HEAD_WIDTH].astype(F32)
    copies[1].wait()
    copies[2].wait()
    small[2].wait()
    lax.fori_loop(0, EARLY, resident, 0, unroll=4)

    pl.semaphore_wait(barrier, n - 1)

    def send(src, dst, s_sem, r_sem, target):
        pltpu.make_async_remote_copy(
            src_ref=src,
            dst_ref=dst,
            send_sem=s_sem,
            recv_sem=r_sem,
            device_id=target,
            device_id_type=pl.DeviceIdType.MESH,
        ).start()

    def send_lists(y, c):
        send(
            msg_ref.at[y * ctx_count + c],
            idx_recv.at[mine],
            send_sem.at[0],
            recv_sem.at[0],
            (y * 2 + my_core, c),
        )

    @pl.loop(0, ctx_count - 1)
    def _(k):
        for y in range(y_count):
            send_lists(y, far_first(k, ctx_count, my_c))

    for k in range(1, y_count):
        send_lists(lax.rem(my_y + k, y_count), my_c)

    for i in range(2):
        send(
            pool_hbm.at[:, i],
            (pk, pv)[i].at[my_core],
            pool_send_sem.at[i],
            pool_recv_sem.at[i],
            pair,
        )

    for k in range(1, y_count):
        y = lax.rem(my_y + k, y_count)
        for i in range(KEY_VALUE_HEADS):
            kv = far_first(i, KEY_VALUE_HEADS, my_c // c_per_kv)
            cols = pl.ds(pl.multiple_of(kv * kv_out, kv_out), kv_out)
            send(
                q_hbm.at[:, cols],
                q_all.at[my_y, :, cols],
                q_send_sem,
                q_recv_sem.at[my_y, kv],
                (y * 2 + my_core, my_c),
            )

    for copy in copies[7:]:
        copy.start()

    idx_recv[mine] = msg_ref[mine]
    copies[3].wait()
    copies[4].wait()
    lax.fori_loop(EARLY, req, resident, 0, unroll=4)

    wait_bytes(idx_recv.at[pl.ds(0, same_core - 1)], recv_sem.at[0])
    lane = lax.broadcasted_iota(jnp.int32, (page_count, LANES), 1)
    page_id = (lax.broadcasted_iota(jnp.int32, (page_count, LANES), 0) + 1).astype(F32)
    spread = (
        lax.broadcasted_iota(jnp.int32, (tokens, page_count), 0) // page_tokens
        == lax.broadcasted_iota(jnp.int32, (tokens, page_count), 1)
    ).astype(F32).astype(BF16)

    def make_bias(y):
        for core in range(2):
            def add(c, count):
                row = idx_recv[y * ctx_count + c, core : core + 1, :]
                return count + (jnp.broadcast_to(row, page_id.shape) == page_id).astype(F32)

            count = lax.fori_loop(0, ctx_count, add, jnp.zeros((page_count, LANES), F32), unroll=8)
            level = jnp.where(
                count > 0.0, jnp.log(jnp.maximum(count, 1.0)) * (1.0 / SCALE), VERY_NEGATIVE
            )
            hi = level.astype(BF16).astype(F32)
            rest = jnp.where(count > 0.0, level - hi, 0.0)
            mid = rest.astype(BF16).astype(F32)
            low = rest - mid
            part = jnp.where(lane < req, hi, jnp.where(lane < 2 * req, mid, low))
            part = jnp.where(lane < 3 * req, part, 0.0).astype(BF16)
            bias[y, core * tokens : (core + 1) * tokens, :] = jnp.dot(
                spread, part, preferred_element_type=F32
            ).astype(BF16)

    copies[5].wait()
    copies[6].wait()
    wait_bytes(pk.at[0], pool_recv_sem.at[0])
    wait_bytes(pv.at[0], pool_recv_sem.at[1])
    rows = per_kv * req
    row_t = lax.rem(lax.broadcasted_iota(jnp.int32, (rows, LANES), 0), req)
    row_lane = lax.broadcasted_iota(jnp.int32, (rows, LANES), 1)
    chooser = (
        ((lax.rem(row_lane, req) == row_t) & (row_lane < 3 * req)).astype(F32).astype(BF16)
    )
    st_lane = lax.broadcasted_iota(jnp.int32, (req, LANES), 1)

    def encode(stat):
        hi = stat.astype(BF16).astype(F32)
        rest = stat - hi
        mid = rest.astype(BF16).astype(F32)
        low = rest - mid
        return (hi + pltpu.roll(mid, PARTS_APART, 1) + pltpu.roll(low, 2 * PARTS_APART, 1)).astype(BF16)

    def decode(block):
        x = block.astype(F32)
        return (
            x + pltpu.roll(x, LANES - PARTS_APART, 1) + pltpu.roll(x, LANES - 2 * PARTS_APART, 1)
        )

    def pool_scores(y, kv):
        qk = jnp.concatenate(
            [
                q_all[
                    y,
                    :,
                    pl.ds(pl.multiple_of((kv * per_kv + h) * HEAD_WIDTH, HEAD_WIDTH), HEAD_WIDTH),
                ]
                for h in range(per_kv)
            ],
            axis=0,
        )
        kv_cols = pl.ds(pl.multiple_of(kv * HEAD_WIDTH, HEAD_WIDTH), HEAD_WIDTH)
        qa = jnp.concatenate([qk, chooser], axis=1)
        ka = jnp.concatenate(
            [pk[:, :, :, kv_cols].reshape(2 * tokens, HEAD_WIDTH), bias[y]], axis=1
        )
        s = lax.dot_general(qa, ka, NT, preferred_element_type=F32)
        return s, jnp.max(s, axis=1, keepdims=True)

    def pool_values(kv, s, m):
        kv_cols = pl.ds(pl.multiple_of(kv * HEAD_WIDTH, HEAD_WIDTH), HEAD_WIDTH)
        p = jnp.exp2((s - m) * (SCALE * LOG2E)).astype(BF16)
        va = jnp.concatenate(
            [
                pv[:, :, :, kv_cols].reshape(2 * tokens, HEAD_WIDTH),
                jnp.ones((2 * tokens, LANES), BF16),
            ],
            axis=1,
        )
        o = jnp.dot(p, va, preferred_element_type=F32)
        top = jnp.broadcast_to(m * (SCALE * LOG2E), (rows, LANES))
        return o[:, :HEAD_WIDTH], o[:, HEAD_WIDTH:], top

    def of_head(x, h):
        return x[h * req : (h + 1) * req, :]

    my_kv = my_c // c_per_kv

    def finish_other(y, kv, o, total, top):
        o = o / total
        lse = top + jnp.log(total) * LOG2E
        stat = jnp.zeros((req, LANES), F32)
        for h in range(per_kv):
            yo_send[kv, y, :, h * HEAD_WIDTH : (h + 1) * HEAD_WIDTH] = of_head(o, h).astype(BF16)
            stat = jnp.where(st_lane == h, of_head(lse, h), stat)
        yo_send[kv, y, :, kv_out:] = encode(stat)
        send(
            yo_send.at[kv, y],
            yo_recv.at[kv, my_y],
            yo_send_sem.at[kv],
            yo_recv_sem.at[kv],
            (y * 2 + my_core, my_c),
        )

    def finish_own(kv, o, total, top, last):
        wait_bytes(yo_recv.at[kv, pl.ds(0, y_count - 1)], yo_recv_sem.at[kv])
        others = []
        for k in range(1, y_count):
            y = lax.rem(my_y + k, y_count)
            others.append((y, decode(yo_recv[kv, y, :, kv_out:])))
        for b in range(c_per_kv):
            c = kv * c_per_kv + b
            stat = jnp.zeros((req, LANES), F32)
            for j in range(heads_each):
                h = b * heads_each + j
                terms = [
                    (of_head(top, h), of_head(total, h), of_head(o, h)),
                    (l_res[:, kv * per_kv + h, :], None, o_res[:, kv * per_kv + h, :]),
                ]
                for y, l_y in others:
                    o_y = yo_recv[kv, y, :, h * HEAD_WIDTH : (h + 1) * HEAD_WIDTH].astype(F32)
                    terms.append((jnp.broadcast_to(l_y[:, h : h + 1], (req, LANES)), None, o_y))
                best = functools.reduce(jnp.maximum, [t[0] for t in terms])
                weights = [jnp.exp2(t[0] - best) for t in terms]
                mass = sum(w if t[1] is None else w * t[1] for w, t in zip(weights, terms))
                o_h = sum(w * t[2] for w, t in zip(weights, terms)) / mass
                l_h = best + jnp.log(mass) * LOG2E
                o_send[c, :, j * HEAD_WIDTH : (j + 1) * HEAD_WIDTH] = o_h.astype(BF16)
                stat = jnp.where(st_lane == j, l_h, stat)
            o_send[c, :, own_width:] = encode(stat)
        for b in range(1 if last else 0, c_per_kv):
            c = kv * c_per_kv + (lax.rem(my_c + b, c_per_kv) if last else b)
            send(o_send.at[c], o_recv.at[my_c], send_sem.at[1], recv_sem.at[1], (my_g, c))

    units = [(k, i) for k in (*range(1, y_count), 0) for i in range(KEY_VALUE_HEADS)]
    places = [
        (lax.rem(my_y + k, y_count), far_first(i, KEY_VALUE_HEADS, my_kv)) for k, i in units
    ]

    def scores_of(u):
        y, kv = places[u]
        if units[u][0]:
            wait_bytes(q_all.at[y, :, pl.ds(0, kv_out)], q_recv_sem.at[y, kv])
        return pool_scores(y, kv)

    make_bias(places[0][0])
    scores = scores_of(0)
    for k in (*range(2, y_count), 0):
        make_bias(lax.rem(my_y + k, y_count))
    for u, (k, i) in enumerate(units):
        y, kv = places[u]
        following = scores_of(u + 1) if u + 1 < len(units) else None
        part = pool_values(kv, *scores)
        scores = following
        if k:
            finish_other(y, kv, *part)
        else:
            finish_own(kv, *part, i == KEY_VALUE_HEADS - 1)

    o_recv[my_c] = o_send[my_c]
    wait_bytes(o_recv.at[pl.ds(0, ctx_count - 1)], recv_sem.at[1])

    def highest(i, top):
        level = decode(o_recv[i, :, own_width:])
        mix_w[i] = level
        return jnp.maximum(top, level)

    top = lax.fori_loop(0, ctx_count, highest, jnp.full((req, LANES), -3e38, F32), unroll=8)

    def weigh(i, total):
        w = jnp.exp2(mix_w[i] - top)
        mix_w[i] = w
        return total + w

    total = lax.fori_loop(0, ctx_count, weigh, jnp.zeros((req, LANES), F32), unroll=8)
    inverse = 1.0 / total

    def join(i, acc):
        w = mix_w[i] * inverse
        return tuple(
            acc[j]
            + w[:, j : j + 1] * o_recv[i, :, j * HEAD_WIDTH : (j + 1) * HEAD_WIDTH].astype(F32)
            for j in range(heads_each)
        )

    acc = lax.fori_loop(
        0,
        ctx_count,
        join,
        tuple(jnp.zeros((req, HEAD_WIDTH), F32) for _ in range(heads_each)),
        unroll=8,
    )
    attn = jnp.concatenate([a.astype(BF16) for a in acc], axis=1)

    copies[7].wait()

    def project(c):
        cols = pl.ds(pl.multiple_of(c * columns, columns), columns)
        return jnp.dot(attn, ow[:, cols], preferred_element_type=F32).astype(BF16)

    @pl.loop(0, ctx_count - 1)
    def _(k):
        c = far_first(k, ctx_count, my_c)
        p_send[c] = project(c)
        send(p_send.at[c], p_recv.at[my_c], send_sem.at[3], recv_sem.at[3], (my_g, c))

    p_recv[my_c] = project(my_c)

    experts = grp_count * EXP_GRP
    places = experts * CAPE
    expert_id = lax.broadcasted_iota(jnp.int32, (experts, req), 0)
    for copy in small[3:]:
        copy.wait()
    taken = jnp.zeros((experts, req), F32)
    table = jnp.zeros((experts, req), F32)
    for k in range(ids_ref.shape[0]):
        match = ids_ref[k : k + 1, :] == expert_id
        taken = taken + jnp.where(match, 1.0, 0.0)
        table = table + jnp.where(match, ew_ref[k : k + 1, :], 0.0)
    before = (
        lax.broadcasted_iota(jnp.int32, (req, req), 0)
        < lax.broadcasted_iota(jnp.int32, (req, req), 1)
    ).astype(F32)
    exact = functools.partial(
        jnp.dot, precision=lax.Precision.HIGHEST, preferred_element_type=F32
    )
    order = exact(taken, before)
    repeat = (
        lax.broadcasted_iota(jnp.int32, (places, experts), 0) // CAPE
        == lax.broadcasted_iota(jnp.int32, (places, experts), 1)
    ).astype(F32)
    slot = lax.rem(lax.broadcasted_iota(jnp.int32, (places, req), 0), CAPE).astype(F32)
    picked = (exact(repeat, taken) > 0.5) & (jnp.abs(exact(repeat, order) - slot) < 0.5)
    picker = picked.astype(F32).astype(BF16)
    gates = jnp.where(picked, exact(repeat, table), 0.0)
    tables = []
    for f in range(0, places, LANES):
        turn[0] = jnp.zeros((LANES, LANES), F32)
        turn[0, :, 0:req] = gates[f : f + LANES, :]
        tables.append(turn[0].T[0:req, :])
    wait_bytes(p_recv.at[pl.ds(0, ctx_count - 1)], recv_sem.at[3])
    hidden = lax.fori_loop(
        0, ctx_count, lambda c, a: a + p_recv[c].astype(F32), res_ref[...].astype(F32)
    )
    outgoing = jnp.dot(picker, hidden.astype(BF16), preferred_element_type=F32)
    for e in range(experts):
        x_send[e] = outgoing[e * CAPE : (e + 1) * CAPE, :].astype(BF16)
    parts_count = ctx_count // EXP_GRP

    def expert_of(d):
        return (d // ctx_count) * EXP_GRP + lax.rem(d, ctx_count) // parts_count

    def dispatch(g, c):
        send(
            x_send.at[expert_of(g * ctx_count + c)],
            x_recv.at[my_c, my_g],
            send_sem.at[4],
            x_recv_sem.at[my_c],
            (g, c),
        )

    @pl.loop(0, ctx_count - 1)
    def _(k):
        for g in range(grp_count):
            dispatch(g, far_first(k, ctx_count, my_c))

    for k in range(1, grp_count):
        dispatch(lax.rem(my_g + k, grp_count), my_c)
    x_recv[my_c, my_g] = x_send[expert_of(me)]

    for i in range(8, 10):
        copies[i].wait()
    units = wg.shape[0]
    width = wg.shape[1]
    slots = grp_count * CAPE

    def gate_up(c, carry):
        squares, gate, up = carry
        cols = pl.ds(pl.multiple_of(c * columns, columns), columns)
        x = jnp.concatenate([x_recv[c, g].astype(F32) for g in range(grp_count)], axis=0)
        squares = squares + jnp.sum(x * x, axis=1, keepdims=True)
        x = (x * gain_ref[:, cols]).astype(BF16)
        gate = gate + lax.dot_general(x, wg[:, cols], NT, preferred_element_type=F32)
        up = up + lax.dot_general(x, wu[:, cols], NT, preferred_element_type=F32)
        return squares, gate, up

    def arrived(k, carry):
        c = far_first(ctx_count - 1 - k, ctx_count, my_c)
        wait_bytes(x_recv.at[c], x_recv_sem.at[c])
        return gate_up(c, carry)

    wait_bytes(x_recv.at[my_c, pl.ds(0, grp_count - 1)], x_recv_sem.at[my_c])
    nothing = jnp.zeros((slots, units), F32)
    carry = gate_up(my_c, (jnp.zeros((slots, 1), F32), nothing, nothing))
    squares, gate, up = lax.fori_loop(1, ctx_count, arrived, carry)
    factor = lax.rsqrt(squares * (1.0 / width) + NORM_EPSILON)
    gate = gate * factor
    up = up * factor
    act = (gate / (1.0 + jnp.exp(-gate)) * up).astype(BF16)
    copies[10].wait()

    def down(c):
        cols = pl.ds(pl.multiple_of(c * columns, columns), columns)
        y = jnp.dot(act, wd[:, cols], preferred_element_type=F32)
        for g in range(grp_count):
            y_send[g * ctx_count + c] = y[g * CAPE : (g + 1) * CAPE, :].astype(BF16)

    def give_back(g, c):
        send(y_send.at[g * ctx_count + c], y_recv.at[me], send_sem.at[5], recv_sem.at[5], (g, c))

    @pl.loop(0, ctx_count - 1)
    def _(k):
        c = far_first(k, ctx_count, my_c)
        down(c)
        for g in range(grp_count):
            give_back(g, c)

    down(my_c)
    for k in range(1, grp_count):
        give_back(lax.rem(my_g + k, grp_count), my_c)
    y_recv[me] = y_send[me]
    wait_bytes(y_recv.at[pl.ds(0, n - 1)], recv_sem.at[5])
    for e in range(experts):
        first = e * parts_count
        y = y_recv[first].astype(F32)
        for part in range(1, parts_count):
            y = y + y_recv[first + part].astype(F32)
        ys[e * CAPE : (e + 1) * CAPE, :] = y
    out = hidden
    for f, gates in enumerate(tables):
        out = out + exact(gates, ys[f * LANES : (f + 1) * LANES, :])
    out_ref[...] = out.astype(BF16)

    wait_bytes(idx_recv.at[pl.ds(0, same_core - 1)], send_sem.at[0])
    wait_bytes(q_all.at[pl.ds(0, y_count - 1)], q_send_sem)
    wait_bytes(pk.at[0], pool_send_sem.at[0])
    wait_bytes(pv.at[0], pool_send_sem.at[1])
    for kv in range(KEY_VALUE_HEADS):
        wait_bytes(yo_send.at[kv, pl.ds(0, y_count - 1)], yo_send_sem.at[kv])
    wait_bytes(o_send.at[pl.ds(0, ctx_count - 1)], send_sem.at[1])
    wait_bytes(p_send.at[pl.ds(0, ctx_count - 1)], send_sem.at[3])
    wait_bytes(y_recv.at[pl.ds(0, n - 1)], send_sem.at[4])
    wait_bytes(y_send.at[pl.ds(0, n - 1)], send_sem.at[5])


def shards(
    queries,
    resident_key_cache,
    resident_value_cache,
    res_len,
    visual_page_pool,
    recall_holder,
    recall_slot,
    o_weight,
    residual,
    norm_gain,
    expert_ids,
    expert_weights,
    w_gate,
    w_up,
    w_down,
):
    ctx_count = lax.axis_size("ctx")
    grp_count = lax.axis_size("grp")
    n = ctx_count * grp_count
    req, q_width = queries.shape
    heads = q_width // HEAD_WIDTH
    y_count = grp_count // 2
    kv_out = q_width // KEY_VALUE_HEADS
    own_width = o_weight.shape[0]
    pages, _, page_tokens, kv_width = visual_page_pool.shape
    tokens = pages * page_tokens
    width = residual.shape[1]
    columns = width // ctx_count
    units = w_gate.shape[1]
    rows_here = resident_key_cache.shape[1]

    vmem = pl.BlockSpec(memory_space=pltpu.VMEM)
    hbm = pl.BlockSpec(memory_space=pl.ANY)
    return pl.pallas_call(
        functools.partial(kernel, grp_count, ctx_count, page_tokens),
        out_shape=pltpu.VMEM((req, columns), BF16),
        in_specs=[hbm] * 15,
        out_specs=vmem,
        scratch_shapes=[
            pltpu.SMEM(res_len.shape, jnp.int32),
            pltpu.VMEM(recall_holder.shape[1:], jnp.int32),
            pltpu.VMEM(recall_slot.shape[1:], jnp.int32),
            pltpu.VMEM((req, columns), BF16),
            pltpu.VMEM((1, width), F32),
            pltpu.VMEM(expert_ids.shape[::-1], jnp.int32),
            pltpu.VMEM(expert_weights.shape[::-1], F32),
            pltpu.VMEM((y_count, req, q_width), BF16),
            pltpu.VMEM((req, heads, HEAD_WIDTH), F32),
            pltpu.VMEM((req, rows_here, kv_width), BF16),
            pltpu.VMEM((req, rows_here, kv_width), BF16),
            pltpu.VMEM((2, pages, page_tokens, kv_width), BF16),
            pltpu.VMEM((2, pages, page_tokens, kv_width), BF16),
            pltpu.VMEM(o_weight.shape, BF16),
            pltpu.VMEM((units, width), BF16),
            pltpu.VMEM((units, width), BF16),
            pltpu.VMEM((units, width), BF16),
            pltpu.VMEM((2, LANES, LANES), F32),
            pltpu.VMEM((n, LANES), F32),
            pltpu.VMEM((y_count * ctx_count, 2, LANES), F32),
            pltpu.VMEM((y_count * ctx_count, 2, LANES), F32),
            pltpu.VMEM((y_count, 2 * tokens, LANES), BF16),
            pltpu.VMEM((req, heads, HEAD_WIDTH), F32),
            pltpu.VMEM((req, heads, HEAD_WIDTH), F32),
            pltpu.VMEM((KEY_VALUE_HEADS, y_count, req, kv_out + LANES), BF16),
            pltpu.VMEM((KEY_VALUE_HEADS, y_count, req, kv_out + LANES), BF16),
            pltpu.VMEM((ctx_count, req, own_width + LANES), BF16),
            pltpu.VMEM((ctx_count, req, own_width + LANES), BF16),
            pltpu.VMEM((ctx_count, req, LANES), F32),
            pltpu.VMEM((ctx_count, req, columns), BF16),
            pltpu.VMEM((ctx_count, req, columns), BF16),
            pltpu.VMEM((grp_count * EXP_GRP, CAPE, columns), BF16),
            pltpu.VMEM((ctx_count, grp_count, CAPE, columns), BF16),
            pltpu.VMEM((n, CAPE, columns), BF16),
            pltpu.VMEM((n, CAPE, columns), BF16),
            pltpu.VMEM((grp_count * EXP_GRP * CAPE, columns), F32),
            pltpu.SemaphoreType.DMA((11,)),
            pltpu.SemaphoreType.DMA((7,)),
            pltpu.SemaphoreType.DMA,
            pltpu.SemaphoreType.DMA((y_count, KEY_VALUE_HEADS)),
            pltpu.SemaphoreType.DMA((2,)),
            pltpu.SemaphoreType.DMA((2,)),
            pltpu.SemaphoreType.DMA((KEY_VALUE_HEADS,)),
            pltpu.SemaphoreType.DMA((KEY_VALUE_HEADS,)),
            pltpu.SemaphoreType.DMA((ctx_count,)),
            pltpu.SemaphoreType.DMA((6,)),
            pltpu.SemaphoreType.DMA((6,)),
        ],
        compiler_params=pltpu.CompilerParams(
            collective_id=0, has_side_effects=True, vmem_limit_bytes=60 * 1024 * 1024
        ),
    )(
        queries,
        resident_key_cache,
        resident_value_cache,
        res_len,
        visual_page_pool,
        recall_holder[0],
        recall_slot[0],
        o_weight,
        residual,
        norm_gain.reshape(1, width),
        expert_ids.T,
        expert_weights.T,
        w_gate,
        w_up,
        w_down,
    )


def solution(mesh):
    placed = (
        P("grp", None),
        P("grp", "ctx", None),
        P("grp", "ctx", None),
        P("grp"),
        P(("grp", "ctx"), None, None, None),
        P("ctx", "grp", None),
        P("ctx", "grp", None),
        P("ctx", None),
        P("grp", None),
        P(),
        P("grp", None),
        P("grp", None),
        P(("grp", "ctx"), None, None),
        P(("grp", "ctx"), None, None),
        P(("grp", "ctx"), None, None),
    )
    return jax.shard_map(
        shards, mesh=mesh, in_specs=placed, out_specs=P("grp", "ctx"), check_vma=False
    )
```

```python
import functools

import jax
import jax.numpy as jnp
from jax import lax
from jax.experimental import pallas as pl
from jax.experimental.pallas import tpu as pltpu
from jax.sharding import PartitionSpec as P

KEY_VALUE_HEADS = 4
HEAD_WIDTH = 128
EXP_GRP = 8
LANES = 128
CAPE = 4
PARTS_APART = 32
EARLY = 4

VERY_NEGATIVE = -1e30
NORM_EPSILON = 1e-06
LOG2E = 1.4426950408889634
SCALE = HEAD_WIDTH ** (-0.5)

NT = (((1,), (1,)), ((), ()))
F32 = jnp.float32
BF16 = jnp.bfloat16


def wait_bytes(ref, sem):
    pltpu.make_async_copy(ref, ref, sem).wait()


def kernel(
    grp_count,
    ctx_count,
    page_tokens,
    q_hbm,
    kc_hbm,
    vc_hbm,
    rl_hbm,
    pool_hbm,
    holder_hbm,
    slot_hbm,
    ow_hbm,
    res_hbm,
    gain_hbm,
    ids_hbm,
    ew_hbm,
    wg_hbm,
    wu_hbm,
    wd_hbm,
    out_ref,
    rl_ref,
    holder_ref,
    slot_ref,
    res_ref,
    gain_ref,
    ids_ref,
    ew_ref,
    q_all,
    qt,
    kc,
    vc,
    pk,
    pv,
    ow,
    wg,
    wu,
    wd,
    turn,
    named,
    msg_ref,
    idx_recv,
    bias,
    o_res,
    l_res,
    yo_send,
    yo_recv,
    o_send,
    o_recv,
    mix_w,
    p_send,
    p_recv,
    x_send,
    x_recv,
    y_send,
    y_recv,
    ys,
    local_sem,
    small_sem,
    q_send_sem,
    q_recv_sem,
    pool_send_sem,
    pool_recv_sem,
    yo_send_sem,
    yo_recv_sem,
    x_recv_sem,
    send_sem,
    recv_sem,
):
    n = grp_count * ctx_count
    my_g = lax.axis_index("grp")
    my_c = lax.axis_index("ctx")
    me = my_g * ctx_count + my_c
    y_count = grp_count // 2
    my_y = my_g // 2
    my_core = lax.rem(my_g, 2)
    pair = (my_g + 1 - 2 * my_core, my_c)
    req = q_all.shape[1]
    heads = qt.shape[1]
    per_kv = heads // KEY_VALUE_HEADS
    kv_out = per_kv * HEAD_WIDTH
    own_width = o_send.shape[2] - LANES
    heads_each = own_width // HEAD_WIDTH
    c_per_kv = per_kv // heads_each
    page_count = pk.shape[1]
    tokens = page_count * page_tokens
    columns = p_send.shape[2]
    same_core = y_count * ctx_count
    mine = my_y * ctx_count + my_c

    def dev(d):
        return (d // ctx_count, lax.rem(d, ctx_count))

    def far_first(k, count, at):
        above, below = count - 1 - at, at
        most, least = jnp.maximum(above, below), jnp.minimum(above, below)
        lead = most - least
        j = jnp.maximum(k - lead, 0)
        side = jnp.where(above >= below, 1, -1) * (1 - 2 * lax.rem(j, 2))
        return at + side * jnp.where(k < lead, most - k, least - j // 2)

    early, late = pl.ds(0, EARLY), pl.ds(EARLY, req - EARLY)
    loads = [
        (q_hbm, q_all.at[my_y]),
        (kc_hbm.at[early], kc.at[early]),
        (vc_hbm.at[early], vc.at[early]),
        (kc_hbm.at[late], kc.at[late]),
        (vc_hbm.at[late], vc.at[late]),
        (pool_hbm.at[:, 0], pk.at[my_core]),
        (pool_hbm.at[:, 1], pv.at[my_core]),
        (ow_hbm, ow),
        (wg_hbm.at[0], wg),
        (wu_hbm.at[0], wu),
        (wd_hbm.at[0], wd),
    ]
    copies = [pltpu.make_async_copy(s, d, local_sem.at[i]) for i, (s, d) in enumerate(loads)]
    own_cols = pl.ds(pl.multiple_of(my_c * columns, columns), columns)
    small_loads = [
        (holder_hbm, holder_ref),
        (slot_hbm, slot_ref),
        (rl_hbm, rl_ref),
        (ids_hbm, ids_ref),
        (ew_hbm, ew_ref),
        (res_hbm.at[:, own_cols], res_ref),
        (gain_hbm, gain_ref),
    ]
    small = [pltpu.make_async_copy(s, d, small_sem.at[i]) for i, (s, d) in enumerate(small_loads)]
    for copy in small[:2] + copies[:3] + small[2:3]:
        copy.start()

    barrier = pltpu.get_barrier_semaphore()

    def greet(g, c):
        pl.semaphore_signal(
            barrier, inc=1, device_id=(g, c), device_id_type=pl.DeviceIdType.MESH
        )

    @pl.loop(0, ctx_count - 1)
    def _(k):
        for g in range(grp_count):
            greet(g, far_first(k, ctx_count, my_c))

    for k in range(1, grp_count):
        greet(lax.rem(my_g + k, grp_count), my_c)
    for copy in copies[3:7] + small[3:]:
        copy.start()

    small[0].wait()
    small[1].wait()
    lists = holder_ref.shape[1]
    for i, ref in enumerate((holder_ref, slot_ref)):
        turn[i] = jnp.zeros((LANES, LANES), F32)
        for r in range(3):
            turn[i, r * req : (r + 1) * req, 0:lists] = ref[...].astype(F32)
    holder_t = turn[0].T
    slot_t = turn[1].T
    holder_id = lax.broadcasted_iota(jnp.int32, (n, LANES), 0).astype(F32)
    table = jnp.zeros((n, LANES), F32)
    for j in range(lists):
        table = table + jnp.where(
            holder_t[j : j + 1, :] == holder_id, slot_t[j : j + 1, :] + 1.0, 0.0
        )
    named[...] = table

    @pl.loop(0, same_core)
    def _(i):
        first = (i // ctx_count) * 2 * ctx_count + lax.rem(i, ctx_count)
        msg_ref[i, 0:1, :] = named[pl.ds(first, 1), :]
        msg_ref[i, 1:2, :] = named[pl.ds(first + ctx_count, 1), :]

    rows_here = kc.shape[1]

    def resident(t, carry):
        pos = my_c * rows_here + lax.broadcasted_iota(jnp.int32, (heads, rows_here), 1)
        ok = pos < rl_ref[t]
        s = jnp.concatenate(
            [
                lax.dot_general(
                    qt[t, k * per_kv : (k + 1) * per_kv, :].astype(BF16),
                    kc[t, :, k * HEAD_WIDTH : (k + 1) * HEAD_WIDTH],
                    NT,
                    preferred_element_type=F32,
                )
                for k in range(KEY_VALUE_HEADS)
            ],
            axis=0,
        )
        s = jnp.where(ok, s, VERY_NEGATIVE)
        m = jnp.max(s, axis=1, keepdims=True)
        p = jnp.exp2((s - m) * (SCALE * LOG2E))
        p = jnp.where(ok, p, 0.0)
        total = jnp.maximum(jnp.sum(p, axis=1, keepdims=True), 1e-30)
        pb = p.astype(BF16)
        o = jnp.concatenate(
            [
                jnp.dot(
                    pb[k * per_kv : (k + 1) * per_kv, :],
                    vc[t, :, k * HEAD_WIDTH : (k + 1) * HEAD_WIDTH],
                    preferred_element_type=F32,
                )
                for k in range(KEY_VALUE_HEADS)
            ],
            axis=0,
        )
        o_res[t] = o / total
        lse = m * (SCALE * LOG2E) + jnp.log(total) * LOG2E
        l_res[t] = jnp.broadcast_to(lse, (heads, LANES))
        return carry

    copies[0].wait()
    for h in range(heads):
        qt[:, h, :] = q_all[my_y, :, h * HEAD_WIDTH : (h + 1) * HEAD_WIDTH].astype(F32)
    copies[1].wait()
    copies[2].wait()
    small[2].wait()
    lax.fori_loop(0, EARLY, resident, 0, unroll=4)

    pl.semaphore_wait(barrier, n - 1)

    def send(src, dst, s_sem, r_sem, target):
        pltpu.make_async_remote_copy(
            src_ref=src,
            dst_ref=dst,
            send_sem=s_sem,
            recv_sem=r_sem,
            device_id=target,
            device_id_type=pl.DeviceIdType.MESH,
        ).start()

    def send_lists(y, c):
        send(
            msg_ref.at[y * ctx_count + c],
            idx_recv.at[mine],
            send_sem.at[0],
            recv_sem.at[0],
            (y * 2 + my_core, c),
        )

    @pl.loop(0, ctx_count - 1)
    def _(k):
        for y in range(y_count):
            send_lists(y, far_first(k, ctx_count, my_c))

    for k in range(1, y_count):
        send_lists(lax.rem(my_y + k, y_count), my_c)

    for i in range(2):
        send(
            pool_hbm.at[:, i],
            (pk, pv)[i].at[my_core],
            pool_send_sem.at[i],
            pool_recv_sem.at[i],
            pair,
        )

    for k in range(1, y_count):
        y = lax.rem(my_y + k, y_count)
        for i in range(KEY_VALUE_HEADS):
            kv = far_first(i, KEY_VALUE_HEADS, my_c // c_per_kv)
            cols = pl.ds(pl.multiple_of(kv * kv_out, kv_out), kv_out)
            send(
                q_hbm.at[:, cols],
                q_all.at[my_y, :, cols],
                q_send_sem,
                q_recv_sem.at[my_y, kv],
                (y * 2 + my_core, my_c),
            )

    for copy in copies[7:]:
        copy.start()

    idx_recv[mine] = msg_ref[mine]
    copies[3].wait()
    copies[4].wait()
    lax.fori_loop(EARLY, req, resident, 0, unroll=4)

    wait_bytes(idx_recv.at[pl.ds(0, same_core - 1)], recv_sem.at[0])
    lane = lax.broadcasted_iota(jnp.int32, (page_count, LANES), 1)
    page_id = (lax.broadcasted_iota(jnp.int32, (page_count, LANES), 0) + 1).astype(F32)
    spread = (
        lax.broadcasted_iota(jnp.int32, (tokens, page_count), 0) // page_tokens
        == lax.broadcasted_iota(jnp.int32, (tokens, page_count), 1)
    ).astype(F32).astype(BF16)

    def make_bias(y):
        for core in range(2):
            def add(c, count):
                row = idx_recv[y * ctx_count + c, core : core + 1, :]
                return count + (jnp.broadcast_to(row, page_id.shape) == page_id).astype(F32)

            count = lax.fori_loop(0, ctx_count, add, jnp.zeros((page_count, LANES), F32), unroll=8)
            level = jnp.where(
                count > 0.0, jnp.log(jnp.maximum(count, 1.0)) * (1.0 / SCALE), VERY_NEGATIVE
            )
            hi = level.astype(BF16).astype(F32)
            rest = jnp.where(count > 0.0, level - hi, 0.0)
            mid = rest.astype(BF16).astype(F32)
            low = rest - mid
            part = jnp.where(lane < req, hi, jnp.where(lane < 2 * req, mid, low))
            part = jnp.where(lane < 3 * req, part, 0.0).astype(BF16)
            bias[y, core * tokens : (core + 1) * tokens, :] = jnp.dot(
                spread, part, preferred_element_type=F32
            ).astype(BF16)

    copies[5].wait()
    copies[6].wait()
    wait_bytes(pk.at[0], pool_recv_sem.at[0])
    wait_bytes(pv.at[0], pool_recv_sem.at[1])
    rows = per_kv * req
    row_t = lax.rem(lax.broadcasted_iota(jnp.int32, (rows, LANES), 0), req)
    row_lane = lax.broadcasted_iota(jnp.int32, (rows, LANES), 1)
    chooser = (
        ((lax.rem(row_lane, req) == row_t) & (row_lane < 3 * req)).astype(F32).astype(BF16)
    )
    st_lane = lax.broadcasted_iota(jnp.int32, (req, LANES), 1)

    def encode(stat):
        hi = stat.astype(BF16).astype(F32)
        rest = stat - hi
        mid = rest.astype(BF16).astype(F32)
        low = rest - mid
        return (hi + pltpu.roll(mid, PARTS_APART, 1) + pltpu.roll(low, 2 * PARTS_APART, 1)).astype(BF16)

    def decode(block):
        x = block.astype(F32)
        return (
            x + pltpu.roll(x, LANES - PARTS_APART, 1) + pltpu.roll(x, LANES - 2 * PARTS_APART, 1)
        )

    def pool_scores(y, kv):
        qk = jnp.concatenate(
            [
                q_all[
                    y,
                    :,
                    pl.ds(pl.multiple_of((kv * per_kv + h) * HEAD_WIDTH, HEAD_WIDTH), HEAD_WIDTH),
                ]
                for h in range(per_kv)
            ],
            axis=0,
        )
        kv_cols = pl.ds(pl.multiple_of(kv * HEAD_WIDTH, HEAD_WIDTH), HEAD_WIDTH)
        qa = jnp.concatenate([qk, chooser], axis=1)
        ka = jnp.concatenate(
            [pk[:, :, :, kv_cols].reshape(2 * tokens, HEAD_WIDTH), bias[y]], axis=1
        )
        s = lax.dot_general(qa, ka, NT, preferred_element_type=F32)
        return s, jnp.max(s, axis=1, keepdims=True)

    def pool_values(kv, s, m):
        kv_cols = pl.ds(pl.multiple_of(kv * HEAD_WIDTH, HEAD_WIDTH), HEAD_WIDTH)
        p = jnp.exp2((s - m) * (SCALE * LOG2E)).astype(BF16)
        va = jnp.concatenate(
            [
                pv[:, :, :, kv_cols].reshape(2 * tokens, HEAD_WIDTH),
                jnp.ones((2 * tokens, LANES), BF16),
            ],
            axis=1,
        )
        o = jnp.dot(p, va, preferred_element_type=F32)
        top = jnp.broadcast_to(m * (SCALE * LOG2E), (rows, LANES))
        return o[:, :HEAD_WIDTH], o[:, HEAD_WIDTH:], top

    def of_head(x, h):
        return x[h * req : (h + 1) * req, :]

    my_kv = my_c // c_per_kv

    def finish_other(y, kv, o, total, top):
        o = o / total
        lse = top + jnp.log(total) * LOG2E
        stat = jnp.zeros((req, LANES), F32)
        for h in range(per_kv):
            yo_send[kv, y, :, h * HEAD_WIDTH : (h + 1) * HEAD_WIDTH] = of_head(o, h).astype(BF16)
            stat = jnp.where(st_lane == h, of_head(lse, h), stat)
        yo_send[kv, y, :, kv_out:] = encode(stat)
        send(
            yo_send.at[kv, y],
            yo_recv.at[kv, my_y],
            yo_send_sem.at[kv],
            yo_recv_sem.at[kv],
            (y * 2 + my_core, my_c),
        )

    def finish_own(kv, o, total, top, last):
        wait_bytes(yo_recv.at[kv, pl.ds(0, y_count - 1)], yo_recv_sem.at[kv])
        others = []
        for k in range(1, y_count):
            y = lax.rem(my_y + k, y_count)
            others.append((y, decode(yo_recv[kv, y, :, kv_out:])))
        for b in range(c_per_kv):
            c = kv * c_per_kv + b
            stat = jnp.zeros((req, LANES), F32)
            for j in range(heads_each):
                h = b * heads_each + j
                terms = [
                    (of_head(top, h), of_head(total, h), of_head(o, h)),
                    (l_res[:, kv * per_kv + h, :], None, o_res[:, kv * per_kv + h, :]),
                ]
                for y, l_y in others:
                    o_y = yo_recv[kv, y, :, h * HEAD_WIDTH : (h + 1) * HEAD_WIDTH].astype(F32)
                    terms.append((jnp.broadcast_to(l_y[:, h : h + 1], (req, LANES)), None, o_y))
                best = functools.reduce(jnp.maximum, [t[0] for t in terms])
                weights = [jnp.exp2(t[0] - best) for t in terms]
                mass = sum(w if t[1] is None else w * t[1] for w, t in zip(weights, terms))
                o_h = sum(w * t[2] for w, t in zip(weights, terms)) / mass
                l_h = best + jnp.log(mass) * LOG2E
                o_send[c, :, j * HEAD_WIDTH : (j + 1) * HEAD_WIDTH] = o_h.astype(BF16)
                stat = jnp.where(st_lane == j, l_h, stat)
            o_send[c, :, own_width:] = encode(stat)
        for b in range(1 if last else 0, c_per_kv):
            c = kv * c_per_kv + (lax.rem(my_c + b, c_per_kv) if last else b)
            send(o_send.at[c], o_recv.at[my_c], send_sem.at[1], recv_sem.at[1], (my_g, c))

    units = [(k, i) for k in (*range(1, y_count), 0) for i in range(KEY_VALUE_HEADS)]
    places = [
        (lax.rem(my_y + k, y_count), far_first(i, KEY_VALUE_HEADS, my_kv)) for k, i in units
    ]

    def scores_of(u):
        y, kv = places[u]
        if units[u][0]:
            wait_bytes(q_all.at[y, :, pl.ds(0, kv_out)], q_recv_sem.at[y, kv])
        return pool_scores(y, kv)

    make_bias(places[0][0])
    scores = scores_of(0)
    for k in (*range(2, y_count), 0):
        make_bias(lax.rem(my_y + k, y_count))
    for u, (k, i) in enumerate(units):
        y, kv = places[u]
        following = scores_of(u + 1) if u + 1 < len(units) else None
        part = pool_values(kv, *scores)
        scores = following
        if k:
            finish_other(y, kv, *part)
        else:
            finish_own(kv, *part, i == KEY_VALUE_HEADS - 1)

    o_recv[my_c] = o_send[my_c]
    wait_bytes(o_recv.at[pl.ds(0, ctx_count - 1)], recv_sem.at[1])

    def highest(i, top):
        level = decode(o_recv[i, :, own_width:])
        mix_w[i] = level
        return jnp.maximum(top, level)

    top = lax.fori_loop(0, ctx_count, highest, jnp.full((req, LANES), -3e38, F32), unroll=8)

    def weigh(i, total):
        w = jnp.exp2(mix_w[i] - top)
        mix_w[i] = w
        return total + w

    total = lax.fori_loop(0, ctx_count, weigh, jnp.zeros((req, LANES), F32), unroll=8)
    inverse = 1.0 / total

    def join(i, acc):
        w = mix_w[i] * inverse
        return tuple(
            acc[j]
            + w[:, j : j + 1] * o_recv[i, :, j * HEAD_WIDTH : (j + 1) * HEAD_WIDTH].astype(F32)
            for j in range(heads_each)
        )

    acc = lax.fori_loop(
        0,
        ctx_count,
        join,
        tuple(jnp.zeros((req, HEAD_WIDTH), F32) for _ in range(heads_each)),
        unroll=8,
    )
    attn = jnp.concatenate([a.astype(BF16) for a in acc], axis=1)

    copies[7].wait()

    def project(c):
        cols = pl.ds(pl.multiple_of(c * columns, columns), columns)
        return jnp.dot(attn, ow[:, cols], preferred_element_type=F32).astype(BF16)

    @pl.loop(0, ctx_count - 1)
    def _(k):
        c = far_first(k, ctx_count, my_c)
        p_send[c] = project(c)
        send(p_send.at[c], p_recv.at[my_c], send_sem.at[3], recv_sem.at[3], (my_g, c))

    p_recv[my_c] = project(my_c)

    experts = grp_count * EXP_GRP
    places = experts * CAPE
    expert_id = lax.broadcasted_iota(jnp.int32, (experts, req), 0)
    for copy in small[3:]:
        copy.wait()
    taken = jnp.zeros((experts, req), F32)
    table = jnp.zeros((experts, req), F32)
    for k in range(ids_ref.shape[0]):
        match = ids_ref[k : k + 1, :] == expert_id
        taken = taken + jnp.where(match, 1.0, 0.0)
        table = table + jnp.where(match, ew_ref[k : k + 1, :], 0.0)
    before = (
        lax.broadcasted_iota(jnp.int32, (req, req), 0)
        < lax.broadcasted_iota(jnp.int32, (req, req), 1)
    ).astype(F32)
    exact = functools.partial(
        jnp.dot, precision=lax.Precision.HIGHEST, preferred_element_type=F32
    )
    order = exact(taken, before)
    repeat = (
        lax.broadcasted_iota(jnp.int32, (places, experts), 0) // CAPE
        == lax.broadcasted_iota(jnp.int32, (places, experts), 1)
    ).astype(F32)
    slot = lax.rem(lax.broadcasted_iota(jnp.int32, (places, req), 0), CAPE).astype(F32)
    picked = (exact(repeat, taken) > 0.5) & (jnp.abs(exact(repeat, order) - slot) < 0.5)
    picker = picked.astype(F32).astype(BF16)
    gates = jnp.where(picked, exact(repeat, table), 0.0)
    tables = []
    for f in range(0, places, LANES):
        turn[0] = jnp.zeros((LANES, LANES), F32)
        turn[0, :, 0:req] = gates[f : f + LANES, :]
        tables.append(turn[0].T[0:req, :])
    wait_bytes(p_recv.at[pl.ds(0, ctx_count - 1)], recv_sem.at[3])
    hidden = lax.fori_loop(
        0, ctx_count, lambda c, a: a + p_recv[c].astype(F32), res_ref[...].astype(F32)
    )
    outgoing = jnp.dot(picker, hidden.astype(BF16), preferred_element_type=F32)
    for e in range(experts):
        x_send[e] = outgoing[e * CAPE : (e + 1) * CAPE, :].astype(BF16)
    parts_count = ctx_count // EXP_GRP

    def expert_of(d):
        return (d // ctx_count) * EXP_GRP + lax.rem(d, ctx_count) // parts_count

    def dispatch(g, c):
        send(
            x_send.at[expert_of(g * ctx_count + c)],
            x_recv.at[my_c, my_g],
            send_sem.at[4],
            x_recv_sem.at[my_c],
            (g, c),
        )

    @pl.loop(0, ctx_count - 1)
    def _(k):
        for g in range(grp_count):
            dispatch(g, far_first(k, ctx_count, my_c))

    for k in range(1, grp_count):
        dispatch(lax.rem(my_g + k, grp_count), my_c)
    x_recv[my_c, my_g] = x_send[expert_of(me)]

    for i in range(8, 10):
        copies[i].wait()
    units = wg.shape[0]
    width = wg.shape[1]
    slots = grp_count * CAPE

    def gate_up(c, carry):
        squares, gate, up = carry
        cols = pl.ds(pl.multiple_of(c * columns, 2 * columns), 2 * columns)
        x = jnp.concatenate(
            [
                jnp.concatenate([x_recv[c + i, g].astype(F32) for g in range(grp_count)], axis=0)
                for i in range(2)
            ],
            axis=1,
        )
        squares = squares + jnp.sum(x * x, axis=1, keepdims=True)
        x = (x * gain_ref[:, cols]).astype(BF16)
        gate = gate + lax.dot_general(x, wg[:, cols], NT, preferred_element_type=F32)
        up = up + lax.dot_general(x, wu[:, cols], NT, preferred_element_type=F32)
        return squares, gate, up

    half = my_c // 2

    def arrived(k, carry):
        c = 2 * far_first(ctx_count // 2 - 1 - k, ctx_count // 2, half)
        for i in range(2):
            wait_bytes(x_recv.at[c + i], x_recv_sem.at[c + i])
        return gate_up(c, carry)

    wait_bytes(x_recv.at[my_c, pl.ds(0, grp_count - 1)], x_recv_sem.at[my_c])
    beside = my_c + 1 - 2 * lax.rem(my_c, 2)
    wait_bytes(x_recv.at[beside], x_recv_sem.at[beside])
    nothing = jnp.zeros((slots, units), F32)
    carry = gate_up(2 * half, (jnp.zeros((slots, 1), F32), nothing, nothing))
    squares, gate, up = lax.fori_loop(1, ctx_count // 2, arrived, carry)
    factor = lax.rsqrt(squares * (1.0 / width) + NORM_EPSILON)
    gate = gate * factor
    up = up * factor
    act = (gate / (1.0 + jnp.exp(-gate)) * up).astype(BF16)
    copies[10].wait()

    def down(c):
        cols = pl.ds(pl.multiple_of(c * columns, columns), columns)
        y = jnp.dot(act, wd[:, cols], preferred_element_type=F32)
        for g in range(grp_count):
            y_send[g * ctx_count + c] = y[g * CAPE : (g + 1) * CAPE, :].astype(BF16)

    def give_back(g, c):
        send(y_send.at[g * ctx_count + c], y_recv.at[me], send_sem.at[5], recv_sem.at[5], (g, c))

    @pl.loop(0, ctx_count - 1)
    def _(k):
        c = far_first(k, ctx_count, my_c)
        down(c)
        for g in range(grp_count):
            give_back(g, c)

    down(my_c)
    for k in range(1, grp_count):
        give_back(lax.rem(my_g + k, grp_count), my_c)
    y_recv[me] = y_send[me]
    wait_bytes(y_recv.at[pl.ds(0, n - 1)], recv_sem.at[5])
    for e in range(experts):
        first = e * parts_count
        y = y_recv[first].astype(F32)
        for part in range(1, parts_count):
            y = y + y_recv[first + part].astype(F32)
        ys[e * CAPE : (e + 1) * CAPE, :] = y
    out = hidden
    for f, gates in enumerate(tables):
        out = out + exact(gates, ys[f * LANES : (f + 1) * LANES, :])
    out_ref[...] = out.astype(BF16)

    wait_bytes(idx_recv.at[pl.ds(0, same_core - 1)], send_sem.at[0])
    wait_bytes(q_all.at[pl.ds(0, y_count - 1)], q_send_sem)
    wait_bytes(pk.at[0], pool_send_sem.at[0])
    wait_bytes(pv.at[0], pool_send_sem.at[1])
    for kv in range(KEY_VALUE_HEADS):
        wait_bytes(yo_send.at[kv, pl.ds(0, y_count - 1)], yo_send_sem.at[kv])
    wait_bytes(o_send.at[pl.ds(0, ctx_count - 1)], send_sem.at[1])
    wait_bytes(p_send.at[pl.ds(0, ctx_count - 1)], send_sem.at[3])
    wait_bytes(y_recv.at[pl.ds(0, n - 1)], send_sem.at[4])
    wait_bytes(y_send.at[pl.ds(0, n - 1)], send_sem.at[5])


def shards(
    queries,
    resident_key_cache,
    resident_value_cache,
    res_len,
    visual_page_pool,
    recall_holder,
    recall_slot,
    o_weight,
    residual,
    norm_gain,
    expert_ids,
    expert_weights,
    w_gate,
    w_up,
    w_down,
):
    ctx_count = lax.axis_size("ctx")
    grp_count = lax.axis_size("grp")
    n = ctx_count * grp_count
    req, q_width = queries.shape
    heads = q_width // HEAD_WIDTH
    y_count = grp_count // 2
    kv_out = q_width // KEY_VALUE_HEADS
    own_width = o_weight.shape[0]
    pages, _, page_tokens, kv_width = visual_page_pool.shape
    tokens = pages * page_tokens
    width = residual.shape[1]
    columns = width // ctx_count
    units = w_gate.shape[1]
    rows_here = resident_key_cache.shape[1]

    vmem = pl.BlockSpec(memory_space=pltpu.VMEM)
    hbm = pl.BlockSpec(memory_space=pl.ANY)
    return pl.pallas_call(
        functools.partial(kernel, grp_count, ctx_count, page_tokens),
        out_shape=pltpu.VMEM((req, columns), BF16),
        in_specs=[hbm] * 15,
        out_specs=vmem,
        scratch_shapes=[
            pltpu.SMEM(res_len.shape, jnp.int32),
            pltpu.VMEM(recall_holder.shape[1:], jnp.int32),
            pltpu.VMEM(recall_slot.shape[1:], jnp.int32),
            pltpu.VMEM((req, columns), BF16),
            pltpu.VMEM((1, width), F32),
            pltpu.VMEM(expert_ids.shape[::-1], jnp.int32),
            pltpu.VMEM(expert_weights.shape[::-1], F32),
            pltpu.VMEM((y_count, req, q_width), BF16),
            pltpu.VMEM((req, heads, HEAD_WIDTH), F32),
            pltpu.VMEM((req, rows_here, kv_width), BF16),
            pltpu.VMEM((req, rows_here, kv_width), BF16),
            pltpu.VMEM((2, pages, page_tokens, kv_width), BF16),
            pltpu.VMEM((2, pages, page_tokens, kv_width), BF16),
            pltpu.VMEM(o_weight.shape, BF16),
            pltpu.VMEM((units, width), BF16),
            pltpu.VMEM((units, width), BF16),
            pltpu.VMEM((units, width), BF16),
            pltpu.VMEM((2, LANES, LANES), F32),
            pltpu.VMEM((n, LANES), F32),
            pltpu.VMEM((y_count * ctx_count, 2, LANES), F32),
            pltpu.VMEM((y_count * ctx_count, 2, LANES), F32),
            pltpu.VMEM((y_count, 2 * tokens, LANES), BF16),
            pltpu.VMEM((req, heads, HEAD_WIDTH), F32),
            pltpu.VMEM((req, heads, HEAD_WIDTH), F32),
            pltpu.VMEM((KEY_VALUE_HEADS, y_count, req, kv_out + LANES), BF16),
            pltpu.VMEM((KEY_VALUE_HEADS, y_count, req, kv_out + LANES), BF16),
            pltpu.VMEM((ctx_count, req, own_width + LANES), BF16),
            pltpu.VMEM((ctx_count, req, own_width + LANES), BF16),
            pltpu.VMEM((ctx_count, req, LANES), F32),
            pltpu.VMEM((ctx_count, req, columns), BF16),
            pltpu.VMEM((ctx_count, req, columns), BF16),
            pltpu.VMEM((grp_count * EXP_GRP, CAPE, columns), BF16),
            pltpu.VMEM((ctx_count, grp_count, CAPE, columns), BF16),
            pltpu.VMEM((n, CAPE, columns), BF16),
            pltpu.VMEM((n, CAPE, columns), BF16),
            pltpu.VMEM((grp_count * EXP_GRP * CAPE, columns), F32),
            pltpu.SemaphoreType.DMA((11,)),
            pltpu.SemaphoreType.DMA((7,)),
            pltpu.SemaphoreType.DMA,
            pltpu.SemaphoreType.DMA((y_count, KEY_VALUE_HEADS)),
            pltpu.SemaphoreType.DMA((2,)),
            pltpu.SemaphoreType.DMA((2,)),
            pltpu.SemaphoreType.DMA((KEY_VALUE_HEADS,)),
            pltpu.SemaphoreType.DMA((KEY_VALUE_HEADS,)),
            pltpu.SemaphoreType.DMA((ctx_count,)),
            pltpu.SemaphoreType.DMA((6,)),
            pltpu.SemaphoreType.DMA((6,)),
        ],
        compiler_params=pltpu.CompilerParams(
            collective_id=0, has_side_effects=True, vmem_limit_bytes=60 * 1024 * 1024
        ),
    )(
        queries,
        resident_key_cache,
        resident_value_cache,
        res_len,
        visual_page_pool,
        recall_holder[0],
        recall_slot[0],
        o_weight,
        residual,
        norm_gain.reshape(1, width),
        expert_ids.T,
        expert_weights.T,
        w_gate,
        w_up,
        w_down,
    )


def solution(mesh):
    placed = (
        P("grp", None),
        P("grp", "ctx", None),
        P("grp", "ctx", None),
        P("grp"),
        P(("grp", "ctx"), None, None, None),
        P("ctx", "grp", None),
        P("ctx", "grp", None),
        P("ctx", None),
        P("grp", None),
        P(),
        P("grp", None),
        P("grp", None),
        P(("grp", "ctx"), None, None),
        P(("grp", "ctx"), None, None),
        P(("grp", "ctx"), None, None),
    )
    return jax.shard_map(
        shards, mesh=mesh, in_specs=placed, out_specs=P("grp", "ctx"), check_vma=False
    )
```
